32 devices in a mesh: wide: 8 (over y, x, core), narrow: 4 (over z).
Axes of the slice: x: 2, y: 2, z: 4, core: 2. Of those that a mesh axis runs over, the one named last changes fastest.
Arguments:
- activity: bfloat16 [32, 8, 512, 512], P(('wide', 'narrow')), may hold values from 0 to 1
- tile_coords: int32 [32, 2], replicated, may hold values from 0 to 7, as said below
- user_owner: int32 [8], replicated, may hold values from 0 to 7, each once
- item_owner: int32 [8], replicated, may hold values from 0 to 7, each once
- user_factor: float32 [4096, 256], P('wide', 'narrow'), may hold values from 0 to 1
- item_factor: float32 [4096, 256], P('wide', 'narrow'), may hold values from 0 to 1
- time_factor: float32 [8, 256], replicated, may hold values from 0.0003 to 0.003
- user_dual: float32 [4096, 256], P('wide', 'narrow'), may hold values from -1.8 to 1.8
- item_dual: float32 [4096, 256], P('wide', 'narrow'), may hold values from -1.8 to 1.8
Outputs:
- new_users: float32 [4096, 256], P('wide', 'narrow')
- new_items: float32 [4096, 256], P('wide', 'narrow')
- new_user_dual: float32 [4096, 256], P('wide', 'narrow')
- new_item_dual: float32 [4096, 256], P('wide', 'narrow')
The draws below stay inside these ranges and needn't reach their ends.
Inputs may be any that keep to these rules, and one draw needn't show every extreme that they name: `tile_coords`: no pair of blocks appears twice. `user_owner`: each stored row block holds exactly one user block. `item_owner`: each stored row block holds exactly one item block.
All inputs are finite; a program needn't handle non-finite values.
Results may differ from the reference program's by a relative error of at most 0.0017.
The reference program's roundings to bfloat16 on the way count: a program that leaves them out, or rounds other values in their place, can miss the bound.
Values may be sent and summed in bfloat16 or wider, within the bound.
No kernel may reach another device: no remote copies, remote signals or barrier semaphores. Data moves between devices by JAX's collectives and lax.ppermute only.
A program may use at most 64 MiB of HBM per device.

```python
import math
import jax
import jax.numpy as jnp
from jax import lax

RANK = 256
BLOCK = 512
TIMES = 8
PASSES = 2
BLOCKS = 8
TILES = 32


def draw_tile_coords(key, part):
    chosen = jax.random.permutation(jax.random.fold_in(key, 11), BLOCKS * BLOCKS)[:TILES]
    return jnp.stack([chosen // BLOCKS, chosen % BLOCKS], axis=1).astype(jnp.int32)


def block_levels(rng, dims, cuts, smallest, high):
    level, own = 1.0, jax.random.fold_in(rng, 6)
    for dim, blocks in cuts:
        heights = jnp.exp(jax.random.uniform(jax.random.fold_in(own, dim), (blocks,), jnp.float32, smallest / len(cuts), high / len(cuts)))
        level = level * jnp.repeat(heights, dims[dim] // blocks).reshape([-1 if axis == dim else 1 for axis in range(len(dims))])
    return level


def bell_draw(key, shape, width, bound, split=(), kind=jnp.bfloat16):
    entries = width * jax.random.normal(key, shape, jnp.float32)
    if split:
        entries = entries * block_levels(key, shape, split, -0.22, 0.18)
    return jnp.clip(entries, -bound, bound).astype(kind)


def setup_inputs(seed: int = 0) -> dict:
    streams_of = jax.random.split(jax.random.key(seed), 10)
    return {
        "activity": jnp.clip(1.0 * jax.random.uniform(streams_of[0], (TILES, TIMES, BLOCK, BLOCK), jnp.float32) ** block_levels(streams_of[0], (TILES, TIMES, BLOCK, BLOCK), ((0, 32),), -0.2, 0.2), 0.0, 1.0).astype(jnp.bfloat16),
        "tile_coords": draw_tile_coords(jax.random.fold_in(streams_of[9], 71), 0),
        "user_owner": jax.random.permutation(streams_of[2], BLOCKS).astype(jnp.int32),
        "item_owner": jax.random.permutation(streams_of[3], BLOCKS).astype(jnp.int32),
        "user_factor": jnp.clip(1.0 * jax.random.uniform(streams_of[4], (BLOCKS * BLOCK, RANK), jnp.float32) ** block_levels(streams_of[4], (BLOCKS * BLOCK, RANK), ((0, 8), (1, 4)), -0.2, 0.2), 0.0, 1.0),
        "item_factor": jnp.clip(1.0 * jax.random.uniform(streams_of[5], (BLOCKS * BLOCK, RANK), jnp.float32) ** block_levels(streams_of[5], (BLOCKS * BLOCK, RANK), ((0, 8), (1, 4)), -0.2, 0.2), 0.0, 1.0),
        "time_factor": jnp.clip(jnp.exp(jax.random.uniform(streams_of[6], (TIMES, RANK), jnp.float32, math.log(0.0003), math.log(0.003))), 0.0003, 0.003),
        "user_dual": bell_draw(streams_of[7], (BLOCKS * BLOCK, RANK), 0.3, 1.8, ((0, 8), (1, 4)), jnp.float32),
        "item_dual": bell_draw(streams_of[8], (BLOCKS * BLOCK, RANK), 0.3, 1.8, ((0, 8), (1, 4)), jnp.float32),
    }


def sums_for(activity, other, time_factor, own_pos, other_pos, forward):
    lowered = other.astype(jnp.bfloat16).reshape(BLOCKS, BLOCK, RANK)

    def add_tile(total, inputs):
        tile, own_block, other_block = inputs
        picked = lax.dynamic_index_in_dim(lowered, other_block, 0, keepdims=False)
        khatri = (picked.astype(jnp.float32)[None] * time_factor[:, None, :]).astype(jnp.bfloat16)
        tile_wide = tile.astype(jnp.float32)
        khatri_wide = khatri.astype(jnp.float32)
        if forward:
            partial_value = jnp.einsum('kij,kjr->ir', tile_wide, khatri_wide, precision=lax.Precision.HIGHEST)
        else:
            partial_value = jnp.einsum('kij,kir->jr', tile_wide, khatri_wide, precision=lax.Precision.HIGHEST)
        return (total.at[own_block].add(partial_value), None)
    start = jnp.zeros((BLOCKS, BLOCK, RANK), jnp.float32)
    total, _ = lax.scan(add_tile, start, (activity, own_pos, other_pos))
    return total.reshape(BLOCKS * BLOCK, RANK)

def admm_update(sums, factor, dual, other, time_factor):
    gram = jnp.dot(other.T, other, precision=lax.Precision.HIGHEST)
    gram = gram * jnp.dot(time_factor.T, time_factor, precision=lax.Precision.HIGHEST)
    penalty = jnp.trace(gram) / RANK
    identity = jnp.eye(RANK, dtype=jnp.float32)
    lower = jnp.linalg.cholesky(gram + penalty * identity)
    inverse = jax.scipy.linalg.cho_solve((lower, True), identity)
    for _ in range(PASSES):
        target = jnp.dot(sums + penalty * (factor + dual), inverse, precision=lax.Precision.HIGHEST)
        factor = jnp.maximum(target - dual, 0.0)
        dual = dual + factor - target
    return (factor, dual)

def reference(activity, tile_coords, user_owner, item_owner, user_factor, item_factor, time_factor, user_dual, item_dual):
    user_pos = user_owner[tile_coords[:, 0]].astype(jnp.int32)
    item_pos = item_owner[tile_coords[:, 1]].astype(jnp.int32)
    user_sums = sums_for(activity, item_factor, time_factor, user_pos, item_pos, True)
    new_users, new_user_dual = admm_update(user_sums, user_factor, user_dual, item_factor, time_factor)
    item_sums = sums_for(activity, new_users, time_factor, item_pos, user_pos, False)
    new_items, new_item_dual = admm_update(item_sums, item_factor, item_dual, new_users, time_factor)
    return (new_users, new_items, new_user_dual, new_item_dual)
```

```python
import functools

import jax
import jax.numpy as jnp
from jax import lax
from jax.experimental import pallas as pl
from jax.experimental.pallas import tpu as pltpu
from jax.sharding import PartitionSpec as P

PASSES = 2
LEAF = 8
HIGHEST = lax.Precision.HIGHEST


def eliminate(left, right):
    panel, width = left.shape
    lane = lax.broadcasted_iota(jnp.int32, (LEAF, width), 1)
    sub = lax.broadcasted_iota(jnp.int32, (LEAF, width), 0)
    for j in range(0, panel, LEAF):
        cols = [jnp.broadcast_to(left[:, j + m : j + m + 1], (panel, width)) for m in range(LEAF)]
        d = [c[j : j + LEAF] for c in cols]
        for k in range(LEAF):
            r = 1.0 / d[k][k : k + 1]
            pivot = d[k]
            here = sub == k
            for m in range(LEAF):
                if m != k:
                    f = d[m][k : k + 1] * r
                    d[m] = jnp.where(here, f, d[m] - pivot * f)
            d[k] = jnp.where(here, r, -pivot * r)
        inside = (lane >= j) & (lane < j + LEAF)
        el = jnp.where(inside, jnp.where(lane == sub + j, 1.0, 0.0), left[j : j + LEAF])
        er = right[j : j + LEAF]
        rl = sum(d[m] * el[m : m + 1] for m in range(LEAF))
        rr = sum(d[m] * er[m : m + 1] for m in range(LEAF))
        new_left, new_right = [], []
        for i in range(0, panel, LEAF):
            if i == j:
                new_left.append(rl)
                new_right.append(rr)
            else:
                c = [col[i : i + LEAF] for col in cols]
                ul = sum(c[m] * rl[m : m + 1] for m in range(LEAF))
                ur = sum(c[m] * rr[m : m + 1] for m in range(LEAF))
                new_left.append(jnp.where(inside, 0.0, left[i : i + LEAF]) - ul)
                new_right.append(right[i : i + LEAF] - ur)
        left = jnp.concatenate(new_left, 0)
        right = jnp.concatenate(new_right, 0)
    return left, right


def inverse_kernel(panel, total_ref, time_ref, inverse_ref, penalty_ref, work_ref):
    rank = total_ref.shape[0]
    half = rank // 2
    time = time_ref[...]
    times = lax.dot_general(
        time, time, (((0,), (0,)), ((), ())), precision=HIGHEST, preferred_element_type=jnp.float32
    )
    gram = total_ref[...] * times
    row = lax.broadcasted_iota(jnp.int32, (rank, rank), 0)
    col = lax.broadcasted_iota(jnp.int32, (rank, rank), 1)
    trace = jnp.sum(jnp.where(row == col, gram, 0.0), axis=0, keepdims=True)
    penalty = jnp.sum(trace, axis=1, keepdims=True) / rank
    penalty_ref[...] = jnp.broadcast_to(penalty, penalty_ref.shape)
    work_ref[...] = gram + jnp.where(row == col, penalty, 0.0)
    lane = lax.broadcasted_iota(jnp.int32, (1, rank), 1)

    def step(k, carry):
        rows = pl.ds(pl.multiple_of(k * panel, panel), panel)
        left, right = eliminate(work_ref[rows, :half], work_ref[rows, half:])
        done = jnp.concatenate([left, right], 1)
        full = work_ref[...]
        change = jnp.dot(
            full[:, :panel], done, precision=HIGHEST, preferred_element_type=jnp.float32
        )
        work_ref[...] = pltpu.roll(jnp.where(lane < panel, 0.0, full) - change, rank - panel, 1)
        work_ref[rows, :] = pltpu.roll(done, rank - panel, 1)
        return carry

    lax.fori_loop(0, rank // panel, step, 0)
    inverse_ref[...] = work_ref[...]


def penalty_inverse(total, time_factor):
    rank = total.shape[0]
    inverse, penalty = pl.pallas_call(
        functools.partial(inverse_kernel, rank // 2),
        out_shape=(
            jax.ShapeDtypeStruct((rank, rank), jnp.float32),
            jax.ShapeDtypeStruct((1, 128), jnp.float32),
        ),
        scratch_shapes=[pltpu.VMEM((rank, rank), jnp.float32)],
        cost_estimate=pl.CostEstimate(
            flops=60_000_000, bytes_accessed=12 * rank * rank, transcendentals=0
        ),
        name="penalty_inverse",
    )(total, time_factor)
    return penalty[0, 0], inverse


def locate(owner, wanted_blocks):
    everyone = jnp.arange(owner.shape[0], dtype=jnp.int32)
    chosen = jnp.where(everyone[None, :] == wanted_blocks[:, None], owner[None, :], 0)
    return jnp.sum(chosen, axis=1)


def swap(x, mask):
    size = lax.axis_size("wide")
    return lax.ppermute(x, "wide", [(i, i ^ mask) for i in range(size)])


def chip_ids():
    me = lax.axis_index("wide")
    chips = lax.axis_size("wide") // 2
    return [(me ^ (2 * m), me ^ (2 * m) ^ 1) for m in range(chips)]


def fetch_rows(lowered, wanted, concat_axis):
    ids = chip_ids()
    same = [lowered] + [swap(lowered, 2 * m) for m in range(1, len(ids))]
    other = [swap(x, 1) for x in same]
    picked = []
    for s in range(wanted.shape[0]):
        value = jnp.zeros_like(lowered)
        for (mine, theirs), a, b in zip(ids, same, other):
            value = jnp.where(wanted[s] == mine, a, value)
            value = jnp.where(wanted[s] == theirs, b, value)
        picked.append(value)
    return lax.all_to_all(
        jnp.stack(picked), "narrow", split_axis=0, concat_axis=concat_axis, tiled=True
    )


def tile_sums(activity, fetched, time_factor, forward):
    khatri = (fetched.astype(jnp.float32)[:, None] * time_factor[None, :, :, None]).astype(
        jnp.bfloat16
    )
    if forward:
        return jnp.einsum("tkij,tkrj->tri", activity, khatri, preferred_element_type=jnp.float32)
    return jnp.einsum("tkij,tkri->trj", activity, khatri, preferred_element_type=jnp.float32)


def owner_sums(partial_value, targets):
    received = lax.all_to_all(partial_value, "narrow", split_axis=2, concat_axis=0, tiled=True)

    def of_block(block):
        return sum(
            jnp.where(targets[s] == block, received[s], 0.0) for s in range(targets.shape[0])
        )

    ids = chip_ids()
    arrived = [swap(of_block(theirs), 1) for _, theirs in ids]
    chip_sums = [of_block(mine) + x for (mine, _), x in zip(ids, arrived)]
    total = chip_sums[0]
    for m in range(1, len(ids)):
        total = total + swap(chip_sums[m], 2 * m)
    return total


def sum_everywhere(local_gram):
    everyone = ("wide", "narrow")
    count = lax.axis_size("wide") * lax.axis_size("narrow")
    rank = local_gram.shape[0]
    parts = lax.all_to_all(local_gram, everyone, split_axis=0, concat_axis=0, tiled=True)
    mine = jnp.sum(parts.reshape(count, rank // count, rank), axis=0)
    copies = jnp.broadcast_to(mine[None], (count, rank // count, rank)).reshape(rank, rank)
    return lax.all_to_all(copies, everyone, split_axis=0, concat_axis=0, tiled=True)


def joint_gram(other, time_factor):
    local_gram = lax.dot_general(other, other, (((1,), (1,)), ((), ())), precision=HIGHEST)
    return penalty_inverse(sum_everywhere(local_gram), time_factor)


def to_rows(x):
    return lax.all_to_all(x, "narrow", split_axis=x.ndim - 1, concat_axis=x.ndim - 2, tiled=True)


def to_columns(x):
    return lax.all_to_all(x, "narrow", split_axis=0, concat_axis=1, tiled=True)


def admm(sums, factor, dual, penalty, inverse):
    shifted = factor + dual
    for _ in range(PASSES):
        target = jnp.dot(inverse, sums + penalty * shifted, precision=HIGHEST)
        value = target - dual
        dual = jnp.maximum(-value, 0.0)
        shifted = jnp.abs(value)
    return value


def local(
    activity,
    tile_coords,
    user_owner,
    item_owner,
    user_factor,
    item_factor,
    time_factor,
    user_dual,
    item_dual,
):
    slots = lax.axis_size("narrow") * activity.shape[0]
    group_coords = lax.dynamic_slice_in_dim(tile_coords, lax.axis_index("wide") * slots, slots, 0)
    user_pos = locate(user_owner, group_coords[:, 0])
    item_pos = locate(item_owner, group_coords[:, 1])
    times_by_rank = time_factor

    item_rows = to_rows(item_factor.T)
    user_rows, udual_rows, idual_rows = to_rows(jnp.stack([user_factor.T, user_dual.T, item_dual.T]))

    fetched = fetch_rows(item_factor.T.astype(jnp.bfloat16), item_pos, 1)
    partial_value = tile_sums(activity, fetched, times_by_rank, True)
    sums = owner_sums(partial_value, user_pos)
    penalty, inverse = joint_gram(item_rows, time_factor)
    value = admm(sums, user_rows, udual_rows, penalty, inverse)

    fresh = jnp.maximum(value, 0.0)
    fetched = fetch_rows(fresh.astype(jnp.bfloat16), user_pos, 2)
    partial_value = tile_sums(activity, fetched, times_by_rank, False)
    sums = owner_sums(partial_value, item_pos)
    penalty, inverse = joint_gram(fresh, time_factor)
    users = to_columns(value).T
    items = to_columns(admm(sums, item_rows, idual_rows, penalty, inverse)).T
    return (
        jnp.maximum(users, 0.0),
        jnp.maximum(items, 0.0),
        jnp.maximum(-users, 0.0),
        jnp.maximum(-items, 0.0),
    )


def solution(mesh):
    in_specs = (
        P(("wide", "narrow"), None, None, None),
        P(),
        P(),
        P(),
        P("wide", "narrow"),
        P("wide", "narrow"),
        P(),
        P("wide", "narrow"),
        P("wide", "narrow"),
    )
    out_specs = (P("wide", "narrow"), P("wide", "narrow"), P("wide", "narrow"), P("wide", "narrow"))
    return jax.shard_map(local, mesh=mesh, in_specs=in_specs, out_specs=out_specs, check_vma=False)
```

```python
import functools

import jax
import jax.numpy as jnp
from jax import lax
from jax.experimental import pallas as pl
from jax.experimental.pallas import tpu as pltpu
from jax.sharding import PartitionSpec as P

PASSES = 2
LEAF = 8
HIGHEST = lax.Precision.HIGHEST
ROOM = pltpu.CompilerParams(vmem_limit_bytes=16 * 2**20)


def eliminate(left, right):
    panel, width = left.shape
    lane = lax.broadcasted_iota(jnp.int32, (LEAF, width), 1)
    sub = lax.broadcasted_iota(jnp.int32, (LEAF, width), 0)
    for j in range(0, panel, LEAF):
        cols = [jnp.broadcast_to(left[:, j + m : j + m + 1], (panel, width)) for m in range(LEAF)]
        d = [c[j : j + LEAF] for c in cols]
        for k in range(LEAF):
            r = 1.0 / d[k][k : k + 1]
            pivot = d[k]
            here = sub == k
            for m in range(LEAF):
                if m != k:
                    f = d[m][k : k + 1] * r
                    d[m] = jnp.where(here, f, d[m] - pivot * f)
            d[k] = jnp.where(here, r, -pivot * r)
        inside = (lane >= j) & (lane < j + LEAF)
        el = jnp.where(inside, jnp.where(lane == sub + j, 1.0, 0.0), left[j : j + LEAF])
        er = right[j : j + LEAF]
        rl = sum(d[m] * el[m : m + 1] for m in range(LEAF))
        rr = sum(d[m] * er[m : m + 1] for m in range(LEAF))
        new_left, new_right = [], []
        for i in range(0, panel, LEAF):
            if i == j:
                new_left.append(rl)
                new_right.append(rr)
            else:
                c = [col[i : i + LEAF] for col in cols]
                ul = sum(c[m] * rl[m : m + 1] for m in range(LEAF))
                ur = sum(c[m] * rr[m : m + 1] for m in range(LEAF))
                new_left.append(jnp.where(inside, 0.0, left[i : i + LEAF]) - ul)
                new_right.append(right[i : i + LEAF] - ur)
        left = jnp.concatenate(new_left, 0)
        right = jnp.concatenate(new_right, 0)
    return left, right


def inverse_kernel(panel, total_ref, time_ref, inverse_ref, penalty_ref, work_ref):
    rank = total_ref.shape[0]
    half = rank // 2
    time = time_ref[...]
    times = lax.dot_general(
        time, time, (((0,), (0,)), ((), ())), precision=HIGHEST, preferred_element_type=jnp.float32
    )
    gram = total_ref[...] * times
    row = lax.broadcasted_iota(jnp.int32, (rank, rank), 0)
    col = lax.broadcasted_iota(jnp.int32, (rank, rank), 1)
    trace = jnp.sum(jnp.where(row == col, gram, 0.0), axis=0, keepdims=True)
    penalty = jnp.sum(trace, axis=1, keepdims=True) / rank
    penalty_ref[...] = jnp.broadcast_to(penalty, penalty_ref.shape)
    work_ref[...] = gram + jnp.where(row == col, penalty, 0.0)
    lane = lax.broadcasted_iota(jnp.int32, (1, rank), 1)

    def step(k, carry):
        rows = pl.ds(pl.multiple_of(k * panel, panel), panel)
        left, right = eliminate(work_ref[rows, :half], work_ref[rows, half:])
        done = jnp.concatenate([left, right], 1)
        full = work_ref[...]
        change = jnp.dot(
            full[:, :panel], done, precision=HIGHEST, preferred_element_type=jnp.float32
        )
        work_ref[...] = pltpu.roll(jnp.where(lane < panel, 0.0, full) - change, rank - panel, 1)
        work_ref[rows, :] = pltpu.roll(done, rank - panel, 1)
        return carry

    lax.fori_loop(0, rank // panel, step, 0)
    inverse_ref[...] = work_ref[...]


def penalty_inverse(total, time_factor):
    rank = total.shape[0]
    inverse, penalty = pl.pallas_call(
        functools.partial(inverse_kernel, rank // 2),
        out_shape=(
            jax.ShapeDtypeStruct((rank, rank), jnp.float32),
            jax.ShapeDtypeStruct((1, 128), jnp.float32),
        ),
        scratch_shapes=[pltpu.VMEM((rank, rank), jnp.float32)],
        cost_estimate=pl.CostEstimate(
            flops=60_000_000, bytes_accessed=12 * rank * rank, transcendentals=0
        ),
        compiler_params=ROOM,
        name="penalty_inverse",
    )(total, time_factor)
    return penalty, inverse


def kernel_call(kernel, name, out_shape, *args, scratch=(), flops=1_000_000, smem=False):
    spec = pl.BlockSpec(memory_space=pltpu.SMEM) if smem else pl.BlockSpec(memory_space=pltpu.VMEM)
    size = sum(x.size * x.dtype.itemsize for x in (*args, *out_shape))
    return pl.pallas_call(
        kernel,
        out_shape=tuple(out_shape),
        in_specs=[spec] * len(args),
        out_specs=tuple(pl.BlockSpec(memory_space=pltpu.VMEM) for _ in out_shape),
        scratch_shapes=list(scratch),
        compiler_params=ROOM,
        cost_estimate=pl.CostEstimate(flops=flops, bytes_accessed=size, transcendentals=0),
        name=name,
    )(*args)


def shape(dims, dtype=jnp.float32):
    return jax.ShapeDtypeStruct(tuple(dims), dtype)


def swap(x, axis, mask):
    size = lax.axis_size(axis)
    return lax.ppermute(x, axis, [(i, i ^ mask) for i in range(size)])


def swaps(pieces):
    return [pieces[0]] + [swap(pieces[d], "narrow", d) for d in range(1, len(pieces))]


def for_each_position(body):
    me = lax.axis_index("narrow")
    for v in range(lax.axis_size("narrow")):
        pl.when(me == v)(functools.partial(body, v))


def rows_of(d, height):
    return pl.ds(pl.multiple_of((lax.axis_index("narrow") ^ d) * height, height), height)


def positions_kernel(coords_ref, user_ref, item_ref, table_ref):
    wide, narrow = lax.axis_index("wide"), lax.axis_index("narrow")
    count = lax.axis_size("narrow")
    for d in range(count):
        tile = wide * count + (narrow ^ d)
        user = user_ref[coords_ref[tile, 0]] ^ wide
        item = item_ref[coords_ref[tile, 1]] ^ wide
        table_ref[d : d + 1, :] = jnp.full((1, 128), user, jnp.int32)
        table_ref[count + d : count + d + 1, :] = jnp.full((1, 128), item, jnp.int32)


def positions(tile_coords, user_owner, item_owner):
    count = lax.axis_size("narrow")
    (table,) = kernel_call(
        positions_kernel, "positions", [shape((2 * count, 128), jnp.int32)],
        tile_coords, user_owner, item_owner, smem=True,
    )
    return table[:count], table[count:]


def split_kernel(count, *refs):
    inputs, outputs = refs[: -count], refs[-count:]
    width = outputs[0].shape[1]
    height = inputs[0].shape[0]

    def body(v):
        for d, out in enumerate(outputs):
            lanes = slice((v ^ d) * width, ((v ^ d) + 1) * width)
            first = inputs[0][:, lanes]
            if len(inputs) > 1:
                first = first + inputs[1][:, lanes]
            out[:height, :] = first
            for k in range(1, len(inputs)):
                out[k * height : (k + 1) * height, :] = inputs[k][:, lanes]

    for_each_position(body)


def split(*arrays):
    count = lax.axis_size("narrow")
    height, rows = arrays[0].shape
    out = [shape((len(arrays) * height, rows // count))] * count
    return kernel_call(functools.partial(split_kernel, count), "split", out, *arrays)


def gram_kernel(*refs):
    pieces, (rows_ref, gram_ref) = refs[:-2], refs[-2:]
    height = pieces[0].shape[0]
    for d, piece in enumerate(pieces):
        rows_ref[rows_of(d, height), :] = piece[...]
    rows = rows_ref[...]
    gram_ref[...] = lax.dot_general(
        rows, rows, (((1,), (1,)), ((), ())), precision=HIGHEST, preferred_element_type=jnp.float32
    )


def assemble_kernel(*refs):
    factor_ref, pieces, outputs = refs[0], refs[1:-4], refs[-4:]
    height = pieces[0].shape[0] // 3
    for d, piece in enumerate(pieces):
        rows = rows_of(d, height)
        outputs[0][rows, :] = piece[:height]
        outputs[1][rows, :] = piece[height : 2 * height]
        outputs[3][rows, :] = piece[2 * height :]
    outputs[2][...] = factor_ref[...] + outputs[3][...]


def total_kernel(parts_ref, out_ref):
    count, height, rank = parts_ref.shape
    total = parts_ref[0]
    for p in range(1, count):
        total = total + parts_ref[p]
    for p in range(count):
        out_ref[p] = total


def sum_everywhere(local_gram):
    everyone = ("wide", "narrow")
    count = lax.axis_size("wide") * lax.axis_size("narrow")
    rank = local_gram.shape[0]
    parts = lax.all_to_all(local_gram, everyone, split_axis=0, concat_axis=0, tiled=True)
    parts = parts.reshape(count, rank // count, rank)
    (copies,) = kernel_call(total_kernel, "total", [shape(parts.shape)], parts)
    return lax.all_to_all(
        copies.reshape(rank, rank), everyone, split_axis=0, concat_axis=0, tiled=True
    )


def pick_kernel(count, table_ref, *refs):
    blocks, outputs = refs[:-count], refs[-count:]
    for d, out in enumerate(outputs):
        here = table_ref[d : d + 1, :1].astype(jnp.float32).astype(out.dtype)
        here = jnp.broadcast_to(here, out.shape)
        value = blocks[0][...]
        for r in range(1, len(blocks)):
            value = jnp.where(here == r, blocks[r][...], value)
        out[...] = value


def fetch_rows(lowered, table):
    chips = lax.axis_size("wide") // 2
    same = [lowered] + [swap(lowered, "wide", 2 * m) for m in range(1, chips)]
    blocks = [x for a in same for x in (a, swap(a, "wide", 1))]
    count = lax.axis_size("narrow")
    picked = kernel_call(
        functools.partial(pick_kernel, count), "pick", [shape(lowered.shape, lowered.dtype)] * count,
        table, *blocks,
    )
    return swaps(picked)


def tile_kernel(forward, count, activity_ref, time_ref, *refs):
    pieces, outputs, (stage_ref, sums_ref) = refs[:count], refs[count : 2 * count], refs[2 * count :]
    me = lax.axis_index("narrow")
    for d, piece in enumerate(pieces):
        stage_ref[me ^ d] = piece[...]
    low = jnp.concatenate([stage_ref[q] for q in range(count)], axis=0 if forward else 1)
    low = low.astype(jnp.float32)
    total = None
    for k in range(activity_ref.shape[1]):
        khatri = (low * time_ref[:, k : k + 1]).astype(jnp.bfloat16)
        dims = (((1,), (1 if forward else 0,)), ((), ()))
        term = lax.dot_general(khatri, activity_ref[0, k], dims, preferred_element_type=jnp.float32)
        total = term if total is None else total + term
    width = outputs[0].shape[1]
    for q in range(count):
        sums_ref[q] = total[:, q * width : (q + 1) * width]
    for d, out in enumerate(outputs):
        out[...] = sums_ref[me ^ d]


def tile_sums(activity, pieces, time_by_rank, forward):
    count = len(pieces)
    rank = time_by_rank.shape[0]
    _, steps, rows, cols = activity.shape
    width = (rows if forward else cols) // count
    return kernel_call(
        functools.partial(tile_kernel, forward, count), "tile", [shape((rank, width))] * count,
        activity, time_by_rank, *pieces,
        scratch=[
            pltpu.VMEM((count, *pieces[0].shape), jnp.bfloat16),
            pltpu.VMEM((count, rank, width), jnp.float32),
        ],
        flops=2 * rank * steps * rows * cols,
    )


def place_kernel(count, table_ref, *refs):
    received, outputs = refs[:count], refs[count:]
    values = [x[...] for x in received]
    for r, out in enumerate(outputs):
        total = None
        for d, value in enumerate(values):
            here = jnp.broadcast_to(table_ref[d : d + 1, :1] == r, value.shape)
            term = jnp.where(here, value, 0.0)
            total = term if total is None else total + term
        out[...] = total


def owner_sums(partials, table):
    received = swaps(partials)
    size = lax.axis_size("wide")
    placed = kernel_call(
        functools.partial(place_kernel, len(received)), "place", [shape(received[0].shape)] * size,
        table, *received,
    )
    terms = [placed[0], swap(placed[1], "wide", 1)]
    arrived = [swap(placed[2 * m + 1], "wide", 1) for m in range(1, size // 2)]
    for m in range(1, size // 2):
        terms.append(swap(placed[2 * m] + arrived[m - 1], "wide", 2 * m))
    return terms


def update_kernel(terms, count, *refs):
    sums = refs[0][...]
    for term in refs[1:terms]:
        sums = sums + term[...]
    shifted_ref, dual_ref, penalty_ref, inverse_ref = refs[terms : terms + 4]
    outputs = refs[terms + 4 :]
    value_ref = outputs[-1]
    penalty = penalty_ref[:1, :1]
    inverse = inverse_ref[...]
    shifted, dual = shifted_ref[...], dual_ref[...]
    for _ in range(PASSES):
        target = jnp.dot(
            inverse, sums + penalty * shifted, precision=HIGHEST, preferred_element_type=jnp.float32
        )
        value = target - dual
        dual = jnp.maximum(-value, 0.0)
        shifted = jnp.abs(value)
    value_ref[...] = value
    height = outputs[0].shape[0]
    for d in range(count):
        outputs[d][...] = value_ref[rows_of(d, height), :]
    if len(outputs) > count + 1:
        low_ref, gram_ref = outputs[count : count + 2]
        fresh = jnp.maximum(value, 0.0)
        low_ref[...] = fresh.astype(low_ref.dtype)
        gram_ref[...] = lax.dot_general(
            fresh, fresh, (((1,), (1,)), ((), ())),
            precision=HIGHEST, preferred_element_type=jnp.float32,
        )


def admm(terms, shifted, dual, penalty, inverse, more):
    count = lax.axis_size("narrow")
    rank, width = shifted.shape
    out = [shape((rank // count, width))] * count
    if more:
        out += [shape((rank, width), jnp.bfloat16), shape((rank, rank))]
    return kernel_call(
        functools.partial(update_kernel, len(terms), count), "update", out,
        *terms, shifted, dual, penalty, inverse,
        scratch=[pltpu.VMEM((rank, width), jnp.float32)],
        flops=12 * rank * rank * width * PASSES,
    )


def final_kernel(count, *refs):
    pieces, (factor_ref, dual_ref) = refs[:count], refs[count:]
    width = pieces[0].shape[1]

    def body(v):
        for d, piece in enumerate(pieces):
            lanes = slice((v ^ d) * width, ((v ^ d) + 1) * width)
            value = piece[...]
            factor_ref[:, lanes] = jnp.maximum(value, 0.0)
            dual_ref[:, lanes] = jnp.maximum(-value, 0.0)

    for_each_position(body)


def to_columns(pieces):
    received = swaps(pieces)
    height, width = received[0].shape
    count = len(received)
    factor, dual = kernel_call(
        functools.partial(final_kernel, count), "final", [shape((height, count * width))] * 2,
        *received,
    )
    return factor.T, dual.T


def local(
    activity,
    tile_coords,
    user_owner,
    item_owner,
    user_factor,
    item_factor,
    time_factor,
    user_dual,
    item_dual,
):
    rank = time_factor.shape[1]
    time_by_rank = time_factor.T
    low = item_factor.T.astype(jnp.bfloat16)
    user_table, item_table = positions(tile_coords, user_owner, item_owner)

    item_pieces = swaps(split(item_factor.T))
    width = item_pieces[0].shape[1]
    item_rows, gram = kernel_call(
        gram_kernel, "gram", [shape((rank, width)), shape((rank, rank))], *item_pieces,
        flops=12 * rank * rank * width,
    )
    other_pieces = swaps(split(user_factor.T, user_dual.T, item_dual.T))
    user_shifted, udual_rows, item_shifted, idual_rows = kernel_call(
        assemble_kernel, "assemble", [shape((rank, width))] * 4, item_rows, *other_pieces
    )

    partials = tile_sums(activity, fetch_rows(low, item_table), time_by_rank, True)
    terms = owner_sums(partials, user_table)
    penalty, inverse = penalty_inverse(sum_everywhere(gram), time_factor)
    *user_pieces, low, gram = admm(terms, user_shifted, udual_rows, penalty, inverse, True)

    partials = tile_sums(activity, fetch_rows(low, user_table), time_by_rank, False)
    terms = owner_sums(partials, item_table)
    penalty, inverse = penalty_inverse(sum_everywhere(gram), time_factor)
    new_users, new_user_dual = to_columns(user_pieces)
    item_pieces = admm(terms, item_shifted, idual_rows, penalty, inverse, False)
    new_items, new_item_dual = to_columns(item_pieces)
    return (new_users, new_items, new_user_dual, new_item_dual)


def solution(mesh):
    in_specs = (
        P(("wide", "narrow"), None, None, None),
        P(),
        P(),
        P(),
        P("wide", "narrow"),
        P("wide", "narrow"),
        P(),
        P("wide", "narrow"),
        P("wide", "narrow"),
    )
    out_specs = (P("wide", "narrow"), P("wide", "narrow"), P("wide", "narrow"), P("wide", "narrow"))
    return jax.shard_map(local, mesh=mesh, in_specs=in_specs, out_specs=out_specs, check_vma=False)
```

```python
import functools

import jax
import jax.numpy as jnp
from jax import lax
from jax.experimental import pallas as pl
from jax.experimental.pallas import tpu as pltpu
from jax.sharding import PartitionSpec as P


PASSES = 2
LEAF = 8
HIGHEST = lax.Precision.HIGHEST
ROOM = pltpu.CompilerParams(vmem_limit_bytes=16 * 2**20)


def eliminate(left, right):
    panel, width = left.shape
    lane = lax.broadcasted_iota(jnp.int32, (LEAF, width), 1)
    sub = lax.broadcasted_iota(jnp.int32, (LEAF, width), 0)
    for j in range(0, panel, LEAF):
        cols = [jnp.broadcast_to(left[:, j + m : j + m + 1], (panel, width)) for m in range(LEAF)]
        d = [c[j : j + LEAF] for c in cols]
        for k in range(LEAF):
            r = 1.0 / d[k][k : k + 1]
            pivot = d[k]
            here = sub == k
            for m in range(LEAF):
                if m != k:
                    f = d[m][k : k + 1] * r
                    d[m] = jnp.where(here, f, d[m] - pivot * f)
            d[k] = jnp.where(here, r, -pivot * r)
        inside = (lane >= j) & (lane < j + LEAF)
        el = jnp.where(inside, jnp.where(lane == sub + j, 1.0, 0.0), left[j : j + LEAF])
        er = right[j : j + LEAF]
        rl = sum(d[m] * el[m : m + 1] for m in range(LEAF))
        rr = sum(d[m] * er[m : m + 1] for m in range(LEAF))
        new_left, new_right = [], []
        for i in range(0, panel, LEAF):
            if i == j:
                new_left.append(rl)
                new_right.append(rr)
            else:
                c = [col[i : i + LEAF] for col in cols]
                ul = sum(c[m] * rl[m : m + 1] for m in range(LEAF))
                ur = sum(c[m] * rr[m : m + 1] for m in range(LEAF))
                new_left.append(jnp.where(inside, 0.0, left[i : i + LEAF]) - ul)
                new_right.append(right[i : i + LEAF] - ur)
        left = jnp.concatenate(new_left, 0)
        right = jnp.concatenate(new_right, 0)
    return left, right


def eliminate_panel(panel, k, work_ref):
    rank = work_ref.shape[0]
    half = rank // 2
    lane = lax.broadcasted_iota(jnp.int32, (1, rank), 1)
    rows = pl.ds(k * panel, panel)
    left, right = eliminate(work_ref[rows, :half], work_ref[rows, half:])
    done = jnp.concatenate([left, right], 1)
    full = work_ref[...]
    change = jnp.dot(full[:, :panel], done, precision=HIGHEST, preferred_element_type=jnp.float32)
    work_ref[...] = pltpu.roll(jnp.where(lane < panel, 0.0, full) - change, rank - panel, 1)
    work_ref[rows, :] = pltpu.roll(done, rank - panel, 1)


def first_half_kernel(panel, time_ref, *refs):
    pieces, (work_ref, penalty_ref) = refs[:-2], refs[-2:]
    rank = work_ref.shape[0]
    height = pieces[0].shape[0]
    wide = lax.axis_index("wide")
    for r, piece in enumerate(pieces):
        place = wide ^ r
        start = (place % 2) * (rank // 2) + (place // 2) * height
        work_ref[pl.ds(pl.multiple_of(start, height), height), :] = piece[...]
    time = time_ref[...]
    times = lax.dot_general(
        time, time, (((0,), (0,)), ((), ())), precision=HIGHEST, preferred_element_type=jnp.float32
    )
    gram = work_ref[...] * times
    row = lax.broadcasted_iota(jnp.int32, (rank, rank), 0)
    col = lax.broadcasted_iota(jnp.int32, (rank, rank), 1)
    trace = jnp.sum(jnp.where(row == col, gram, 0.0), axis=0, keepdims=True)
    penalty = jnp.sum(trace, axis=1, keepdims=True) / rank
    penalty_ref[...] = jnp.broadcast_to(penalty, penalty_ref.shape)
    work_ref[...] = gram + jnp.where(row == col, penalty, 0.0)
    eliminate_panel(panel, 0, work_ref)


def second_half_kernel(panel, half_ref, inverse_ref):
    inverse_ref[...] = half_ref[...]
    eliminate_panel(panel, 1, inverse_ref)


def penalty_inverse(pieces, time_factor):
    rank = time_factor.shape[1]
    half, penalty = kernel_call(
        functools.partial(first_half_kernel, rank // 2),
        [shape((rank, rank)), shape((1, 128))], time_factor, *pieces, flops=6_000_000_000,
    )
    (inverse,) = kernel_call(
        functools.partial(second_half_kernel, rank // 2),
        [shape((rank, rank))], half, flops=6_000_000_000,
    )
    return penalty, inverse


def kernel_call(kernel, out_shape, *args, scratch=(), flops=1_000_000, smem=False):
    spec = pl.BlockSpec(memory_space=pltpu.SMEM) if smem else pl.BlockSpec(memory_space=pltpu.VMEM)
    size = sum(x.size * x.dtype.itemsize for x in (*args, *out_shape))
    return pl.pallas_call(
        kernel,
        out_shape=tuple(out_shape),
        in_specs=[spec] * len(args),
        out_specs=tuple(pl.BlockSpec(memory_space=pltpu.VMEM) for _ in out_shape),
        scratch_shapes=list(scratch),
        compiler_params=ROOM,
        cost_estimate=pl.CostEstimate(flops=flops, bytes_accessed=size, transcendentals=0),
    )(*args)


def shape(dims, dtype=jnp.float32):
    return jax.ShapeDtypeStruct(tuple(dims), dtype)


def swap(x, axis, mask):
    size = lax.axis_size(axis)
    return lax.ppermute(x, axis, [(i, i ^ mask) for i in range(size)])


def swaps(pieces):
    return [pieces[0]] + [swap(pieces[d], "narrow", d) for d in range(1, len(pieces))]


def for_each_position(body):
    me = lax.axis_index("narrow")
    for v in range(lax.axis_size("narrow")):
        pl.when(me == v)(functools.partial(body, v))


def rows_of(d, height):
    return pl.ds(pl.multiple_of((lax.axis_index("narrow") ^ d) * height, height), height)


def positions_kernel(coords_ref, user_ref, item_ref, table_ref):
    wide, narrow = lax.axis_index("wide"), lax.axis_index("narrow")
    count = lax.axis_size("narrow")
    for d in range(count):
        tile = wide * count + (narrow ^ d)
        user = user_ref[coords_ref[tile, 0]] ^ wide
        item = item_ref[coords_ref[tile, 1]] ^ wide
        table_ref[d : d + 1, :] = jnp.full((1, 128), user, jnp.int32)
        table_ref[count + d : count + d + 1, :] = jnp.full((1, 128), item, jnp.int32)


def positions(tile_coords, user_owner, item_owner):
    count = lax.axis_size("narrow")
    (table,) = kernel_call(
        positions_kernel, [shape((2 * count, 128), jnp.int32)],
        tile_coords, user_owner, item_owner, smem=True,
    )
    return table[:count], table[count:]


def start_kernel(factor_ref, low_ref, *outputs):
    low_ref[...] = factor_ref[...].astype(low_ref.dtype)
    split_kernel(len(outputs), factor_ref, *outputs)


def start(factor):
    count = lax.axis_size("narrow")
    height, rows = factor.shape
    out = [shape(factor.shape, jnp.bfloat16)] + [shape((height, rows // count))] * count
    low, *pieces = kernel_call(start_kernel, out, factor)
    return low, pieces


def split_kernel(count, *refs):
    inputs, outputs = refs[: -count], refs[-count:]
    width = outputs[0].shape[1]
    height = inputs[0].shape[0]

    def body(v):
        for d, out in enumerate(outputs):
            lanes = slice((v ^ d) * width, ((v ^ d) + 1) * width)
            first = inputs[0][:, lanes]
            if len(inputs) > 1:
                first = first + inputs[1][:, lanes]
            out[:height, :] = first
            for k in range(1, len(inputs)):
                out[k * height : (k + 1) * height, :] = inputs[k][:, lanes]

    for_each_position(body)


def split(*arrays):
    count = lax.axis_size("narrow")
    height, rows = arrays[0].shape
    out = [shape((len(arrays) * height, rows // count))] * count
    return kernel_call(functools.partial(split_kernel, count), out, *arrays)


def halves(gram, give_ref, keep_ref):
    half = keep_ref.shape[0]
    for core in range(2):

        @pl.when(lax.axis_index("wide") % 2 == core)
        def _(core=core):
            keep_ref[...] = gram[core * half : (core + 1) * half]
            give_ref[...] = gram[(1 - core) * half : (2 - core) * half]


def gram_of(rows):
    return lax.dot_general(
        rows, rows, (((1,), (1,)), ((), ())), precision=HIGHEST, preferred_element_type=jnp.float32
    )


def gram_kernel(*refs):
    pieces, (rows_ref, give_ref, keep_ref) = refs[:-3], refs[-3:]
    height = pieces[0].shape[0]
    for d, piece in enumerate(pieces):
        rows_ref[rows_of(d, height), :] = piece[...]
    halves(gram_of(rows_ref[...]), give_ref, keep_ref)


def assemble_kernel(*refs):
    factor_ref, pieces, outputs = refs[0], refs[1:-4], refs[-4:]
    height = pieces[0].shape[0] // 3
    for d, piece in enumerate(pieces):
        rows = rows_of(d, height)
        outputs[0][rows, :] = piece[:height]
        outputs[1][rows, :] = piece[height : 2 * height]
        outputs[3][rows, :] = piece[2 * height :]
    outputs[2][...] = factor_ref[...] + outputs[3][...]


def chip_sum_kernel(keep_ref, got_ref, *refs):
    outputs, total_ref = refs[:-1], refs[-1]
    total_ref[...] = keep_ref[...] + got_ref[...]
    height = outputs[0].shape[0]
    chip = lax.axis_index("wide") // 2
    for m, out in enumerate(outputs):
        out[...] = total_ref[pl.ds(pl.multiple_of((chip ^ m) * height, height), height), :]


def sum_kernel(*refs):
    total = refs[0][...]
    for x in refs[1:-1]:
        total = total + x[...]
    refs[-1][...] = total


def add_up(pieces):
    (total,) = kernel_call(sum_kernel, [shape(pieces[0].shape)], *pieces)
    return total


def sum_everywhere(give, keep):
    chips = lax.axis_size("wide") // 2
    half, rank = keep.shape
    got = swap(give, "wide", 1)
    pieces = kernel_call(
        chip_sum_kernel, [shape((half // chips, rank))] * chips, keep, got,
        scratch=[pltpu.VMEM((half, rank), jnp.float32)],
    )
    pieces = [pieces[0]] + [swap(pieces[m], "wide", 2 * m) for m in range(1, chips)]
    mine = add_up(pieces)
    mine = add_up(swaps([mine] * lax.axis_size("narrow")))
    pieces = [mine] + [swap(mine, "wide", 2 * m) for m in range(1, chips)]
    return [x for a in pieces for x in (a, swap(a, "wide", 1))]


def pick_kernel(count, table_ref, *refs):
    blocks, outputs = refs[:-count], refs[-count:]
    for d, out in enumerate(outputs):
        here = table_ref[d : d + 1, :1].astype(jnp.float32).astype(out.dtype)
        here = jnp.broadcast_to(here, out.shape)
        value = blocks[0][...]
        for r in range(1, len(blocks)):
            value = jnp.where(here == r, blocks[r][...], value)
        out[...] = value


def fetch_rows(lowered, table):
    chips = lax.axis_size("wide") // 2
    same = [lowered] + [swap(lowered, "wide", 2 * m) for m in range(1, chips)]
    blocks = [x for a in same for x in (a, swap(a, "wide", 1))]
    count = lax.axis_size("narrow")
    picked = kernel_call(
        functools.partial(pick_kernel, count), [shape(lowered.shape, lowered.dtype)] * count,
        table, *blocks,
    )
    return swaps(picked)


def tile_kernel(forward, count, activity_ref, time_ref, *refs):
    pieces, outputs = refs[:count], refs[count : 2 * count]
    tile_ref, stage_ref, sums_ref, sems = refs[2 * count :]
    steps = activity_ref.shape[1]
    copies = [
        pltpu.make_async_copy(activity_ref.at[0, k], tile_ref.at[k], sems.at[k])
        for k in range(steps)
    ]
    for copy in copies:
        copy.start()
    me = lax.axis_index("narrow")
    for d, piece in enumerate(pieces):
        stage_ref[me ^ d] = piece[...]
    low = jnp.concatenate([stage_ref[q] for q in range(count)], axis=0 if forward else 1)
    low = low.astype(jnp.float32)
    total = None
    for k in range(steps):
        khatri = (low * time_ref[:, k : k + 1]).astype(jnp.bfloat16)
        dims = (((1,), (1 if forward else 0,)), ((), ()))
        copies[k].wait()
        term = lax.dot_general(khatri, tile_ref[k], dims, preferred_element_type=jnp.float32)
        total = term if total is None else total + term
    width = outputs[0].shape[1]
    for q in range(count):
        sums_ref[q] = total[:, q * width : (q + 1) * width]
    for d, out in enumerate(outputs):
        out[...] = sums_ref[me ^ d]


def tile_sums(activity, pieces, time_by_rank, forward):
    count = len(pieces)
    rank = time_by_rank.shape[0]
    _, steps, rows, cols = activity.shape
    width = (rows if forward else cols) // count
    inside = pl.BlockSpec(memory_space=pltpu.VMEM)
    return pl.pallas_call(
        functools.partial(tile_kernel, forward, count),
        out_shape=(shape((rank, width)),) * count,
        in_specs=[pl.BlockSpec(memory_space=pl.ANY)] + [inside] * (count + 1),
        out_specs=(inside,) * count,
        scratch_shapes=[
            pltpu.VMEM(activity.shape[1:], activity.dtype),
            pltpu.VMEM((count, *pieces[0].shape), jnp.bfloat16),
            pltpu.VMEM((count, rank, width), jnp.float32),
            pltpu.SemaphoreType.DMA((steps,)),
        ],
        compiler_params=pltpu.CompilerParams(vmem_limit_bytes=60 * 2**20),
        cost_estimate=pl.CostEstimate(
            flops=2_000_000_000, bytes_accessed=2 * activity.size, transcendentals=0
        ),
        name="tile",
    )(activity, time_by_rank, *pieces)


def place_kernel(count, table_ref, *refs):
    received, outputs = refs[:count], refs[count:]
    values = [x[...] for x in received]
    for r, out in enumerate(outputs):
        total = None
        for d, value in enumerate(values):
            here = jnp.broadcast_to(table_ref[d : d + 1, :1] == r, value.shape)
            term = jnp.where(here, value, 0.0)
            total = term if total is None else total + term
        out[...] = total


def owner_sums(partials, table):
    received = swaps(partials)
    size = lax.axis_size("wide")
    placed = kernel_call(
        functools.partial(place_kernel, len(received)), [shape(received[0].shape)] * size,
        table, *received,
    )
    arrived = [swap(placed[2 * m + 1], "wide", 1) for m in range(1, size // 2)]
    terms = [placed[0], swap(placed[1], "wide", 1)]
    for m in range(1, size // 2):
        terms.append(swap(placed[2 * m] + arrived[m - 1], "wide", 2 * m))
    return terms


def update_kernel(terms, count, *refs):
    sums = refs[0][...]
    for term in refs[1:terms]:
        sums = sums + term[...]
    shifted_ref, dual_ref, penalty_ref, inverse_ref = refs[terms : terms + 4]
    outputs = refs[terms + 4 :]
    value_ref = outputs[-1]
    penalty = penalty_ref[:1, :1]
    inverse = inverse_ref[...]
    shifted, dual = shifted_ref[...], dual_ref[...]
    for _ in range(PASSES):
        target = jnp.dot(
            inverse, sums + penalty * shifted, precision=HIGHEST, preferred_element_type=jnp.float32
        )
        value = target - dual
        dual = jnp.maximum(-value, 0.0)
        shifted = jnp.abs(value)
    value_ref[...] = value
    height = outputs[0].shape[0]
    for d in range(count):
        outputs[d][...] = value_ref[rows_of(d, height), :]
    if len(outputs) > count + 1:
        low_ref, give_ref, keep_ref = outputs[count : count + 3]
        fresh = jnp.maximum(value, 0.0)
        low_ref[...] = fresh.astype(low_ref.dtype)
        halves(gram_of(fresh), give_ref, keep_ref)


def admm(terms, shifted, dual, penalty, inverse, more):
    count = lax.axis_size("narrow")
    rank, width = shifted.shape
    out = [shape((rank // count, width))] * count
    if more:
        out += [shape((rank, width), jnp.bfloat16)] + [shape((rank // 2, rank))] * 2
    return kernel_call(
        functools.partial(update_kernel, len(terms), count), out,
        *terms, shifted, dual, penalty, inverse,
        scratch=[pltpu.VMEM((rank, width), jnp.float32)],
        flops=12 * rank * rank * width * PASSES,
    )


def final_kernel(count, *refs):
    pieces, (factor_ref, dual_ref) = refs[:count], refs[count:]
    width = pieces[0].shape[1]

    def body(v):
        for d, piece in enumerate(pieces):
            lanes = slice((v ^ d) * width, ((v ^ d) + 1) * width)
            value = piece[...]
            factor_ref[:, lanes] = jnp.maximum(value, 0.0)
            dual_ref[:, lanes] = jnp.maximum(-value, 0.0)

    for_each_position(body)


def to_columns(pieces):
    received = swaps(pieces)
    height, width = received[0].shape
    count = len(received)
    factor, dual = kernel_call(
        functools.partial(final_kernel, count), [shape((height, count * width))] * 2,
        *received,
    )
    return factor.T, dual.T


def local(
    activity,
    tile_coords,
    user_owner,
    item_owner,
    user_factor,
    item_factor,
    time_factor,
    user_dual,
    item_dual,
):
    return sweep(
        activity, tile_coords, user_owner, item_owner, user_factor.T, item_factor.T,
        time_factor, user_dual.T, item_dual.T,
    )


def sweep(
    activity, tile_coords, user_owner, item_owner, user_factor, item_factor, time_factor,
    user_dual, item_dual,
):
    rank = time_factor.shape[1]
    time_by_rank = time_factor.T
    low, item_pieces = start(item_factor)
    user_table, item_table = positions(tile_coords, user_owner, item_owner)

    item_pieces = swaps(item_pieces)
    width = item_pieces[0].shape[1]
    item_rows, *gram = kernel_call(
        gram_kernel, [shape((rank, width))] + [shape((rank // 2, rank))] * 2, *item_pieces,
        flops=12 * rank * rank * width,
    )
    other_pieces = swaps(split(user_factor, user_dual, item_dual))
    user_shifted, udual_rows, item_shifted, idual_rows = kernel_call(
        assemble_kernel, [shape((rank, width))] * 4, item_rows, *other_pieces
    )

    partials = tile_sums(activity, fetch_rows(low, item_table), time_by_rank, True)
    terms = owner_sums(partials, user_table)
    penalty, inverse = penalty_inverse(sum_everywhere(*gram), time_factor)
    *user_pieces, low, give, keep = admm(terms, user_shifted, udual_rows, penalty, inverse, True)

    partials = tile_sums(activity, fetch_rows(low, user_table), time_by_rank, False)
    terms = owner_sums(partials, item_table)
    penalty, inverse = penalty_inverse(sum_everywhere(give, keep), time_factor)
    new_users, new_user_dual = to_columns(user_pieces)
    item_pieces = admm(terms, item_shifted, idual_rows, penalty, inverse, False)
    new_items, new_item_dual = to_columns(item_pieces)
    return (new_users, new_items, new_user_dual, new_item_dual)


def solution(mesh):
    in_specs = (
        P(("wide", "narrow"), None, None, None),
        P(),
        P(),
        P(),
        P("wide", "narrow"),
        P("wide", "narrow"),
        P(),
        P("wide", "narrow"),
        P("wide", "narrow"),
    )
    out_specs = (P("wide", "narrow"), P("wide", "narrow"), P("wide", "narrow"), P("wide", "narrow"))
    return jax.shard_map(local, mesh=mesh, in_specs=in_specs, out_specs=out_specs, check_vma=False)
```

```python
import functools

import jax
import jax.numpy as jnp
from jax import lax
from jax.experimental import pallas as pl
from jax.experimental.pallas import tpu as pltpu
from jax.sharding import PartitionSpec as P


PASSES = 2
LEAF = 8
HIGHEST = lax.Precision.HIGHEST
ROOM = pltpu.CompilerParams(vmem_limit_bytes=16 * 2**20)


def eliminate(left, right):
    panel, width = left.shape
    lane = lax.broadcasted_iota(jnp.int32, (LEAF, width), 1)
    sub = lax.broadcasted_iota(jnp.int32, (LEAF, width), 0)
    for j in range(0, panel, LEAF):
        cols = [jnp.broadcast_to(left[:, j + m : j + m + 1], (panel, width)) for m in range(LEAF)]
        d = [c[j : j + LEAF] for c in cols]
        for k in range(LEAF):
            r = 1.0 / d[k][k : k + 1]
            pivot = d[k]
            here = sub == k
            for m in range(LEAF):
                if m != k:
                    f = d[m][k : k + 1] * r
                    d[m] = jnp.where(here, f, d[m] - pivot * f)
            d[k] = jnp.where(here, r, -pivot * r)
        inside = (lane >= j) & (lane < j + LEAF)
        el = jnp.where(inside, jnp.where(lane == sub + j, 1.0, 0.0), left[j : j + LEAF])
        er = right[j : j + LEAF]
        rl = sum(d[m] * el[m : m + 1] for m in range(LEAF))
        rr = sum(d[m] * er[m : m + 1] for m in range(LEAF))
        new_left, new_right = [], []
        for i in range(0, panel, LEAF):
            if i == j:
                new_left.append(rl)
                new_right.append(rr)
            else:
                c = [col[i : i + LEAF] for col in cols]
                ul = sum(c[m] * rl[m : m + 1] for m in range(LEAF))
                ur = sum(c[m] * rr[m : m + 1] for m in range(LEAF))
                new_left.append(jnp.where(inside, 0.0, left[i : i + LEAF]) - ul)
                new_right.append(right[i : i + LEAF] - ur)
        left = jnp.concatenate(new_left, 0)
        right = jnp.concatenate(new_right, 0)
    return left, right


def eliminate_panel(panel, k, work_ref):
    rank = work_ref.shape[0]
    half = rank // 2
    lane = lax.broadcasted_iota(jnp.int32, (1, rank), 1)
    rows = pl.ds(k * panel, panel)
    left, right = eliminate(work_ref[rows, :half], work_ref[rows, half:])
    done = jnp.concatenate([left, right], 1)
    full = work_ref[...]
    change = jnp.dot(full[:, :panel], done, precision=HIGHEST, preferred_element_type=jnp.float32)
    work_ref[...] = pltpu.roll(jnp.where(lane < panel, 0.0, full) - change, rank - panel, 1)
    work_ref[rows, :] = pltpu.roll(done, rank - panel, 1)


def first_half_kernel(panel, time_ref, *refs):
    pieces, (work_ref, penalty_ref) = refs[:-2], refs[-2:]
    rank = work_ref.shape[0]
    height = pieces[0].shape[0]
    wide = lax.axis_index("wide")
    for r, piece in enumerate(pieces):
        place = wide ^ r
        start = (place % 2) * (rank // 2) + (place // 2 % 2) * height
        work_ref[pl.ds(pl.multiple_of(start, height), height), :] = piece[...]
    time = time_ref[...]
    times = lax.dot_general(
        time, time, (((0,), (0,)), ((), ())), precision=HIGHEST, preferred_element_type=jnp.float32
    )
    gram = work_ref[...] * times
    row = lax.broadcasted_iota(jnp.int32, (rank, rank), 0)
    col = lax.broadcasted_iota(jnp.int32, (rank, rank), 1)
    trace = jnp.sum(jnp.where(row == col, gram, 0.0), axis=0, keepdims=True)
    penalty = jnp.sum(trace, axis=1, keepdims=True) / rank
    penalty_ref[...] = jnp.broadcast_to(penalty, penalty_ref.shape)
    work_ref[...] = gram + jnp.where(row == col, penalty, 0.0)
    eliminate_panel(panel, 0, work_ref)


def second_half_kernel(panel, half_ref, inverse_ref):
    inverse_ref[...] = half_ref[...]
    eliminate_panel(panel, 1, inverse_ref)


def penalty_inverse(pieces, time_factor):
    rank = time_factor.shape[1]
    half, penalty = kernel_call(
        functools.partial(first_half_kernel, rank // 2),
        [shape((rank, rank)), shape((1, 128))], time_factor, *pieces, flops=6_000_000_000,
    )
    (inverse,) = kernel_call(
        functools.partial(second_half_kernel, rank // 2),
        [shape((rank, rank))], half, flops=6_000_000_000,
    )
    return penalty, inverse


def kernel_call(kernel, out_shape, *args, scratch=(), flops=1_000_000, smem=False):
    spec = pl.BlockSpec(memory_space=pltpu.SMEM) if smem else pl.BlockSpec(memory_space=pltpu.VMEM)
    size = sum(x.size * x.dtype.itemsize for x in (*args, *out_shape))
    return pl.pallas_call(
        kernel,
        out_shape=tuple(out_shape),
        in_specs=[spec] * len(args),
        out_specs=tuple(pl.BlockSpec(memory_space=pltpu.VMEM) for _ in out_shape),
        scratch_shapes=list(scratch),
        compiler_params=ROOM,
        cost_estimate=pl.CostEstimate(flops=flops, bytes_accessed=size, transcendentals=0),
    )(*args)


def shape(dims, dtype=jnp.float32):
    return jax.ShapeDtypeStruct(tuple(dims), dtype)


def swap(x, axis, mask):
    size = lax.axis_size(axis)
    return lax.ppermute(x, axis, [(i, i ^ mask) for i in range(size)])


def swaps(pieces):
    return [pieces[0]] + [swap(pieces[d], "narrow", d) for d in range(1, len(pieces))]


def for_each_position(body):
    me = lax.axis_index("narrow")
    for v in range(lax.axis_size("narrow")):
        pl.when(me == v)(functools.partial(body, v))


def rows_of(d, height):
    return pl.ds(pl.multiple_of((lax.axis_index("narrow") ^ d) * height, height), height)


def positions_kernel(coords_ref, user_ref, item_ref, table_ref):
    wide, narrow = lax.axis_index("wide"), lax.axis_index("narrow")
    count = lax.axis_size("narrow")
    for d in range(count):
        tile = wide * count + (narrow ^ d)
        user = user_ref[coords_ref[0, tile]] ^ wide
        item = item_ref[coords_ref[1, tile]] ^ wide
        table_ref[d : d + 1, :] = jnp.full((1, 128), user, jnp.int32)
        table_ref[count + d : count + d + 1, :] = jnp.full((1, 128), item, jnp.int32)


def positions(tile_coords, user_owner, item_owner):
    count = lax.axis_size("narrow")
    (table,) = kernel_call(
        positions_kernel, [shape((2 * count, 128), jnp.int32)],
        tile_coords.T, user_owner, item_owner, smem=True,
    )
    return table[:count], table[count:]


def start_kernel(stack_ref, *outputs):
    width = outputs[0].shape[1]

    def body(v):
        for d, out in enumerate(outputs):
            out[...] = stack_ref[:, (v ^ d) * width : ((v ^ d) + 1) * width]

    for_each_position(body)


def start(item_factor, item_dual, user_factor, user_dual):
    count = lax.axis_size("narrow")
    stack = jnp.concatenate([item_factor, user_factor + user_dual, user_dual, item_dual])
    height, rows = stack.shape
    return kernel_call(start_kernel, [shape((height, rows // count))] * count, stack)


def gram_parts(rows, far_ref, near_ref):
    gram = lax.dot_general(
        rows, rows, (((1,), (1,)), ((), ())), precision=HIGHEST, preferred_element_type=jnp.float32
    )
    half = near_ref.shape[0]
    for core in range(2):

        @pl.when(lax.axis_index("wide") % 2 == core)
        def _(core=core):
            near_ref[...] = gram[core * half : (core + 1) * half]
            far_ref[...] = gram[(1 - core) * half : (2 - core) * half]


def gram_kernel(count, *refs):
    pieces, (factor_ref, far_ref, near_ref) = refs[:count], refs[count:]
    height = pieces[0].shape[0] // 4
    for d, piece in enumerate(pieces):
        factor_ref[rows_of(d, height), :] = piece[:height]
    gram_parts(factor_ref[...], far_ref, near_ref)


def assemble_kernel(count, *refs):
    factor_ref, pieces, outputs = refs[0], refs[1 : count + 1], refs[count + 1 :]
    height = pieces[0].shape[0] // 4
    for d, piece in enumerate(pieces):
        rows = rows_of(d, height)
        outputs[0][rows, :] = piece[height : 2 * height]
        outputs[1][rows, :] = piece[2 * height : 3 * height]
        outputs[3][rows, :] = piece[3 * height :]
    outputs[2][...] = factor_ref[...] + outputs[3][...]


def chip_sum_kernel(near_ref, got_ref, far_out, near_out, total_ref):
    total_ref[...] = near_ref[...] + got_ref[...]
    height = near_out.shape[0]
    side = (lax.axis_index("wide") // 2) % 2
    near_out[...] = total_ref[pl.ds(pl.multiple_of(side * height, height), height), :]
    far_out[...] = total_ref[pl.ds(pl.multiple_of((1 - side) * height, height), height), :]


def sum_everywhere(far, near):
    half, rank = near.shape
    got = swap(far, "wide", 1)
    far, near = kernel_call(
        chip_sum_kernel, [shape((half // 2, rank))] * 2, near, got,
        scratch=[pltpu.VMEM((half, rank), jnp.float32)],
    )
    total = near + swap(far, "wide", 2)
    for axis, mask in (("wide", 4), ("narrow", 1)):
        while mask < lax.axis_size(axis):
            total = total + swap(total, axis, mask)
            mask *= 2
    parts = [total, swap(total, "wide", 2)]
    return [x for part in parts for x in (part, swap(part, "wide", 1))]


def pick_kernel(count, table_ref, *refs):
    blocks, outputs = refs[:-count], refs[-count:]
    for d, out in enumerate(outputs):
        here = table_ref[d : d + 1, :1].astype(jnp.float32).astype(out.dtype)
        here = jnp.broadcast_to(here, out.shape)
        value = blocks[0][...]
        for r in range(1, len(blocks)):
            value = jnp.where(here == r, blocks[r][...], value)
        out[...] = value


def fetch_rows(lowered, table):
    chips = lax.axis_size("wide") // 2
    same = [lowered] + [swap(lowered, "wide", 2 * m) for m in range(1, chips)]
    blocks = [x for a in same for x in (a, swap(a, "wide", 1))]
    count = lax.axis_size("narrow")
    picked = kernel_call(
        functools.partial(pick_kernel, count), [shape(lowered.shape, lowered.dtype)] * count,
        table, *blocks, flops=5_000_000_000,
    )
    return swaps(picked)


def tile_kernel(forward, count, activity_ref, time_ref, *refs):
    pieces, outputs, (stage_ref, sums_ref) = refs[:count], refs[count : 2 * count], refs[2 * count :]
    me = lax.axis_index("narrow")
    for d, piece in enumerate(pieces):
        stage_ref[me ^ d] = piece[...]
    low = jnp.concatenate([stage_ref[q] for q in range(count)], axis=0 if forward else 1)
    low = low.astype(jnp.float32)
    times = time_ref[...].T
    total = None
    for k in range(activity_ref.shape[1]):
        khatri = (low * times[:, k : k + 1]).astype(jnp.bfloat16)
        dims = (((1,), (1 if forward else 0,)), ((), ()))
        term = lax.dot_general(khatri, activity_ref[0, k], dims, preferred_element_type=jnp.float32)
        total = term if total is None else total + term
    width = outputs[0].shape[1]
    for q in range(count):
        sums_ref[q] = total[:, q * width : (q + 1) * width]
    for d, out in enumerate(outputs):
        out[...] = sums_ref[me ^ d]


def tile_sums(activity, pieces, time_factor, forward):
    count = len(pieces)
    rank = time_factor.shape[1]
    _, steps, rows, cols = activity.shape
    width = (rows if forward else cols) // count
    return kernel_call(
        functools.partial(tile_kernel, forward, count), [shape((rank, width))] * count,
        activity, time_factor, *pieces,
        scratch=[
            pltpu.VMEM((count, *pieces[0].shape), jnp.bfloat16),
            pltpu.VMEM((count, rank, width), jnp.float32),
        ],
        flops=2 * rank * steps * rows * cols,
    )


def place_kernel(count, table_ref, *refs):
    received, outputs = refs[:count], refs[count:]
    values = [x[...] for x in received]
    for r, out in enumerate(outputs):
        total = None
        for d, value in enumerate(values):
            here = jnp.broadcast_to(table_ref[d : d + 1, :1] == r, value.shape)
            term = jnp.where(here, value, 0.0)
            total = term if total is None else total + term
        out[...] = total


def owner_sums(partials, table):
    received = swaps(partials)
    size = lax.axis_size("wide")
    placed = kernel_call(
        functools.partial(place_kernel, len(received)), [shape(received[0].shape)] * size,
        table, *received,
    )
    arrived = [swap(placed[2 * m + 1], "wide", 1) for m in range(1, size // 2)]
    terms = [placed[0], swap(placed[1], "wide", 1)]
    for m in range(1, size // 2):
        terms.append(swap(placed[2 * m] + arrived[m - 1], "wide", 2 * m))
    return terms


def update_kernel(terms, count, *refs):
    sums = refs[0][...]
    for term in refs[1:terms]:
        sums = sums + term[...]
    shifted_ref, dual_ref, penalty_ref, inverse_ref = refs[terms : terms + 4]
    outputs = refs[terms + 4 :]
    value_ref = outputs[-1]
    penalty = penalty_ref[:1, :1]
    inverse = inverse_ref[...]
    shifted, dual = shifted_ref[...], dual_ref[...]
    for _ in range(PASSES):
        target = jnp.dot(
            inverse, sums + penalty * shifted, precision=HIGHEST, preferred_element_type=jnp.float32
        )
        value = target - dual
        dual = jnp.maximum(-value, 0.0)
        shifted = jnp.abs(value)
    value_ref[...] = value
    height = outputs[0].shape[0]
    for d in range(count):
        outputs[d][...] = value_ref[rows_of(d, height), :]
    if len(outputs) > count + 1:
        low_ref, far_ref, near_ref = outputs[count : count + 3]
        fresh = jnp.maximum(value, 0.0)
        low_ref[...] = fresh.astype(low_ref.dtype)
        gram_parts(fresh, far_ref, near_ref)


def admm(terms, shifted, dual, penalty, inverse, more):
    count = lax.axis_size("narrow")
    rank, width = shifted.shape
    out = [shape((rank // count, width))] * count
    if more:
        out += [shape((rank, width), jnp.bfloat16)] + [shape((rank // 2, rank))] * 2
    return kernel_call(
        functools.partial(update_kernel, len(terms), count), out,
        *terms, shifted, dual, penalty, inverse,
        scratch=[pltpu.VMEM((rank, width), jnp.float32)],
        flops=12 * rank * rank * width * PASSES,
    )


def final_kernel(count, *refs):
    pieces, (factor_ref, dual_ref) = refs[:count], refs[count:]
    width = pieces[0].shape[1]

    def body(v):
        for d, piece in enumerate(pieces):
            lanes = slice((v ^ d) * width, ((v ^ d) + 1) * width)
            value = piece[...]
            factor_ref[:, lanes] = jnp.maximum(value, 0.0)
            dual_ref[:, lanes] = jnp.maximum(-value, 0.0)

    for_each_position(body)


def to_columns(pieces):
    received = swaps(pieces)
    height, width = received[0].shape
    count = len(received)
    factor, dual = kernel_call(
        functools.partial(final_kernel, count), [shape((height, count * width))] * 2,
        *received,
    )
    return factor.T, dual.T


def local(
    activity,
    tile_coords,
    user_owner,
    item_owner,
    user_factor,
    item_factor,
    time_factor,
    user_dual,
    item_dual,
):
    return sweep(
        activity, tile_coords, user_owner, item_owner, user_factor.T, item_factor.T,
        time_factor, user_dual.T, item_dual.T,
    )


def sweep(
    activity, tile_coords, user_owner, item_owner, user_factor, item_factor, time_factor,
    user_dual, item_dual,
):
    rank = time_factor.shape[1]
    count = lax.axis_size("narrow")
    user_table, item_table = positions(tile_coords, user_owner, item_owner)

    pieces = swaps(start(item_factor, item_dual, user_factor, user_dual))
    width = pieces[0].shape[1]
    half = shape((rank // 2, rank))
    item_rows, far, near = kernel_call(
        functools.partial(gram_kernel, count), [shape((rank, width)), half, half], *pieces,
        flops=12 * rank * rank * width,
    )
    user_shifted, udual_rows, item_shifted, idual_rows = kernel_call(
        functools.partial(assemble_kernel, count), [shape((rank, width))] * 4,
        item_rows, *pieces,
    )

    low = item_factor.astype(jnp.bfloat16)
    partials = tile_sums(activity, fetch_rows(low, item_table), time_factor, True)
    terms = owner_sums(partials, user_table)
    penalty, inverse = penalty_inverse(sum_everywhere(far, near), time_factor)
    *user_pieces, low, far, near = admm(terms, user_shifted, udual_rows, penalty, inverse, True)

    partials = tile_sums(activity, fetch_rows(low, user_table), time_factor, False)
    terms = owner_sums(partials, item_table)
    penalty, inverse = penalty_inverse(sum_everywhere(far, near), time_factor)
    new_users, new_user_dual = to_columns(user_pieces)
    item_pieces = admm(terms, item_shifted, idual_rows, penalty, inverse, False)
    new_items, new_item_dual = to_columns(item_pieces)
    return (new_users, new_items, new_user_dual, new_item_dual)


def solution(mesh):
    in_specs = (
        P(("wide", "narrow"), None, None, None),
        P(),
        P(),
        P(),
        P("wide", "narrow"),
        P("wide", "narrow"),
        P(),
        P("wide", "narrow"),
        P("wide", "narrow"),
    )
    out_specs = (P("wide", "narrow"), P("wide", "narrow"), P("wide", "narrow"), P("wide", "narrow"))
    return jax.shard_map(local, mesh=mesh, in_specs=in_specs, out_specs=out_specs, check_vma=False)
```

```python
import functools

import jax
import jax.numpy as jnp
from jax import lax
from jax.experimental import pallas as pl
from jax.experimental.pallas import tpu as pltpu
from jax.sharding import PartitionSpec as P


PASSES = 2
LEAF = 8
HIGHEST = lax.Precision.HIGHEST
ROOM = pltpu.CompilerParams(vmem_limit_bytes=16 * 2**20)


def eliminate(left, right):
    panel, width = left.shape
    lane = lax.broadcasted_iota(jnp.int32, (LEAF, width), 1)
    sub = lax.broadcasted_iota(jnp.int32, (LEAF, width), 0)
    for j in range(0, panel, LEAF):
        cols = [jnp.broadcast_to(left[:, j + m : j + m + 1], (panel, width)) for m in range(LEAF)]
        d = [c[j : j + LEAF] for c in cols]
        for k in range(LEAF):
            r = 1.0 / d[k][k : k + 1]
            pivot = d[k]
            here = sub == k
            for m in range(LEAF):
                if m != k:
                    f = d[m][k : k + 1] * r
                    d[m] = jnp.where(here, f, d[m] - pivot * f)
            d[k] = jnp.where(here, r, -pivot * r)
        inside = (lane >= j) & (lane < j + LEAF)
        el = jnp.where(inside, jnp.where(lane == sub + j, 1.0, 0.0), left[j : j + LEAF])
        er = right[j : j + LEAF]
        rl = sum(d[m] * el[m : m + 1] for m in range(LEAF))
        rr = sum(d[m] * er[m : m + 1] for m in range(LEAF))
        new_left, new_right = [], []
        for i in range(0, panel, LEAF):
            if i == j:
                new_left.append(rl)
                new_right.append(rr)
            else:
                c = [col[i : i + LEAF] for col in cols]
                ul = sum(c[m] * rl[m : m + 1] for m in range(LEAF))
                ur = sum(c[m] * rr[m : m + 1] for m in range(LEAF))
                new_left.append(jnp.where(inside, 0.0, left[i : i + LEAF]) - ul)
                new_right.append(right[i : i + LEAF] - ur)
        left = jnp.concatenate(new_left, 0)
        right = jnp.concatenate(new_right, 0)
    return left, right


def eliminate_panel(panel, k, work_ref):
    rank = work_ref.shape[0]
    half = rank // 2
    lane = lax.broadcasted_iota(jnp.int32, (1, rank), 1)
    rows = pl.ds(k * panel, panel)
    left, right = eliminate(work_ref[rows, :half], work_ref[rows, half:])
    done = jnp.concatenate([left, right], 1)
    full = work_ref[...]
    change = jnp.dot(full[:, :panel], done, precision=HIGHEST, preferred_element_type=jnp.float32)
    work_ref[...] = pltpu.roll(jnp.where(lane < panel, 0.0, full) - change, rank - panel, 1)
    work_ref[rows, :] = pltpu.roll(done, rank - panel, 1)


def first_half_kernel(panel, time_ref, *refs):
    pieces, (work_ref, penalty_ref) = refs[:-2], refs[-2:]
    rank = work_ref.shape[0]
    half = rank // 2
    for r, piece in enumerate(pieces):
        start = (lax.axis_index("wide") % 2 ^ r) * half
        work_ref[pl.ds(pl.multiple_of(start, half), half), :] = piece[...]
    time = time_ref[...]
    times = lax.dot_general(
        time, time, (((0,), (0,)), ((), ())), precision=HIGHEST, preferred_element_type=jnp.float32
    )
    gram = work_ref[...] * times
    row = lax.broadcasted_iota(jnp.int32, (rank, rank), 0)
    col = lax.broadcasted_iota(jnp.int32, (rank, rank), 1)
    trace = jnp.sum(jnp.where(row == col, gram, 0.0), axis=0, keepdims=True)
    penalty = jnp.sum(trace, axis=1, keepdims=True) / rank
    penalty_ref[...] = jnp.broadcast_to(penalty, penalty_ref.shape)
    work_ref[...] = gram + jnp.where(row == col, penalty, 0.0)
    eliminate_panel(panel, 0, work_ref)


def second_half_kernel(panel, half_ref, inverse_ref):
    inverse_ref[...] = half_ref[...]
    eliminate_panel(panel, 1, inverse_ref)


def penalty_inverse(pieces, time_factor):
    rank = time_factor.shape[1]
    half, penalty = kernel_call(
        functools.partial(first_half_kernel, rank // 2),
        [shape((rank, rank)), shape((1, 128))], time_factor, *pieces, flops=6_000_000_000,
    )
    (inverse,) = kernel_call(
        functools.partial(second_half_kernel, rank // 2),
        [shape((rank, rank))], half, flops=6_000_000_000,
    )
    return penalty, inverse


def kernel_call(kernel, out_shape, *args, scratch=(), flops=1_000_000, smem=False):
    spec = pl.BlockSpec(memory_space=pltpu.SMEM) if smem else pl.BlockSpec(memory_space=pltpu.VMEM)
    size = sum(x.size * x.dtype.itemsize for x in (*args, *out_shape))
    return pl.pallas_call(
        kernel,
        out_shape=tuple(out_shape),
        in_specs=[spec] * len(args),
        out_specs=tuple(pl.BlockSpec(memory_space=pltpu.VMEM) for _ in out_shape),
        scratch_shapes=list(scratch),
        compiler_params=ROOM,
        cost_estimate=pl.CostEstimate(flops=flops, bytes_accessed=size, transcendentals=0),
    )(*args)


def shape(dims, dtype=jnp.float32):
    return jax.ShapeDtypeStruct(tuple(dims), dtype)


def swap(x, axis, mask):
    size = lax.axis_size(axis)
    return lax.ppermute(x, axis, [(i, i ^ mask) for i in range(size)])


def swaps(pieces):
    return [pieces[0]] + [swap(pieces[d], "narrow", d) for d in range(1, len(pieces))]


def for_each_position(body):
    me = lax.axis_index("narrow")
    for v in range(lax.axis_size("narrow")):
        pl.when(me == v)(functools.partial(body, v))


def rows_of(d, height):
    return pl.ds(pl.multiple_of((lax.axis_index("narrow") ^ d) * height, height), height)


def positions_kernel(coords_ref, user_ref, item_ref, table_ref):
    wide, narrow = lax.axis_index("wide"), lax.axis_index("narrow")
    count = lax.axis_size("narrow")
    for d in range(count):
        tile = wide * count + (narrow ^ d)
        user = user_ref[coords_ref[0, tile]] ^ wide
        item = item_ref[coords_ref[1, tile]] ^ wide
        table_ref[d : d + 1, :] = jnp.full((1, 128), user, jnp.int32)
        table_ref[count + d : count + d + 1, :] = jnp.full((1, 128), item, jnp.int32)


def positions(tile_coords, user_owner, item_owner):
    count = lax.axis_size("narrow")
    (table,) = kernel_call(
        positions_kernel, [shape((2 * count, 128), jnp.int32)],
        tile_coords.T, user_owner, item_owner, smem=True,
    )
    return table[:count], table[count:]


def split_kernel(stack_ref, *outputs):
    width = outputs[0].shape[1]

    def body(v):
        for d, out in enumerate(outputs):
            out[...] = stack_ref[:, (v ^ d) * width : ((v ^ d) + 1) * width]

    for_each_position(body)


def split(stack):
    count = lax.axis_size("narrow")
    height, rows = stack.shape
    return kernel_call(split_kernel, [shape((height, rows // count))] * count, stack)


def store_pair(value, pair_ref):
    rank = value.shape[0]
    rounded = value.astype(pair_ref.dtype)
    pair_ref[:rank] = rounded
    pair_ref[rank:] = (value - rounded.astype(jnp.float32)).astype(pair_ref.dtype)


def pair_kernel(count, *refs):
    pieces, (factor_ref, pair_ref) = refs[:count], refs[count:]
    height = pieces[0].shape[0]
    for d, piece in enumerate(pieces):
        factor_ref[rows_of(d, height), :] = piece[...]
    store_pair(factor_ref[...], pair_ref)


def assemble_kernel(count, *refs):
    factor_ref, pieces, outputs = refs[0], refs[1 : count + 1], refs[count + 1 :]
    height = pieces[0].shape[0] // 3
    for d, piece in enumerate(pieces):
        rows = rows_of(d, height)
        outputs[0][rows, :] = piece[:height]
        outputs[1][rows, :] = piece[height : 2 * height]
        outputs[3][rows, :] = piece[2 * height :]
    outputs[2][...] = factor_ref[...] + outputs[3][...]


def gram_kernel(*refs):
    pairs, (half_ref, rows_ref) = refs[:-2], refs[-2:]
    rank = rows_ref.shape[0]
    width = pairs[0].shape[1]
    for k, pair in enumerate(pairs):
        rows_ref[:, k * width : (k + 1) * width] = pair[:rank].astype(jnp.float32) + pair[
            rank:
        ].astype(jnp.float32)
    half = half_ref.shape[0]
    start = pl.multiple_of(lax.axis_index("wide") % 2 * half, half)
    half_ref[...] = lax.dot_general(
        rows_ref[pl.ds(start, half), :], rows_ref[...], (((1,), (1,)), ((), ())),
        precision=HIGHEST, preferred_element_type=jnp.float32,
    )


def joint_gram(pairs):
    rank, width = pairs[0].shape[0] // 2, pairs[0].shape[1]
    (total,) = kernel_call(
        gram_kernel, [shape((rank // 2, rank))], *pairs,
        scratch=[pltpu.VMEM((rank, len(pairs) * width), jnp.float32)],
        flops=1_500_000_000,
    )
    mask = 1
    while mask < lax.axis_size("narrow"):
        total = total + swap(total, "narrow", mask)
        mask *= 2
    return total, swap(total, "wide", 1)


def pick_kernel(count, table_ref, *refs):
    pairs, outputs = refs[:-count], refs[-count:]
    for d, out in enumerate(outputs):
        rank = out.shape[0]
        here = table_ref[d : d + 1, :1].astype(jnp.float32).astype(out.dtype)
        here = jnp.broadcast_to(here, out.shape)
        value = pairs[0][:rank]
        for r in range(1, len(pairs)):
            value = jnp.where(here == r, pairs[r][:rank], value)
        out[...] = value


def all_pairs(pair):
    chips = lax.axis_size("wide") // 2
    same = [pair] + [swap(pair, "wide", 2 * m) for m in range(1, chips)]
    return [x for a in same for x in (a, swap(a, "wide", 1))]


def fetch_rows(pairs, table):
    count = lax.axis_size("narrow")
    rank, width = pairs[0].shape[0] // 2, pairs[0].shape[1]
    picked = kernel_call(
        functools.partial(pick_kernel, count), [shape((rank, width), jnp.bfloat16)] * count,
        table, *pairs, flops=5_000_000_000,
    )
    return swaps(picked)


def tile_kernel(forward, count, activity_ref, time_ref, *refs):
    pieces, outputs, (stage_ref, sums_ref) = refs[:count], refs[count : 2 * count], refs[2 * count :]
    me = lax.axis_index("narrow")
    for d, piece in enumerate(pieces):
        stage_ref[me ^ d] = piece[...]
    low = jnp.concatenate([stage_ref[q] for q in range(count)], axis=1)
    low = low.astype(jnp.float32)
    times = time_ref[...].T
    total = None
    for k in range(activity_ref.shape[1]):
        khatri = (low * times[:, k : k + 1]).astype(jnp.bfloat16)
        dims = (((1,), (1 if forward else 0,)), ((), ()))
        term = lax.dot_general(khatri, activity_ref[0, k], dims, preferred_element_type=jnp.float32)
        total = term if total is None else total + term
    width = outputs[0].shape[1]
    for q in range(count):
        sums_ref[q] = total[:, q * width : (q + 1) * width]
    for d, out in enumerate(outputs):
        out[...] = sums_ref[me ^ d]


def tile_sums(activity, pieces, time_factor, forward):
    count = len(pieces)
    rank = time_factor.shape[1]
    _, steps, rows, cols = activity.shape
    width = (rows if forward else cols) // count
    return kernel_call(
        functools.partial(tile_kernel, forward, count), [shape((rank, width))] * count,
        activity, time_factor, *pieces,
        scratch=[
            pltpu.VMEM((count, *pieces[0].shape), jnp.bfloat16),
            pltpu.VMEM((count, rank, width), jnp.float32),
        ],
        flops=2 * rank * steps * rows * cols,
    )


def place_kernel(count, table_ref, *refs):
    received, outputs = refs[:count], refs[count:]
    values = [x[...] for x in received]
    for r, out in enumerate(outputs):
        total = None
        for d, value in enumerate(values):
            here = jnp.broadcast_to(table_ref[d : d + 1, :1] == r, value.shape)
            term = jnp.where(here, value, 0.0)
            total = term if total is None else total + term
        out[...] = total


def owner_sums(partials, table):
    received = swaps(partials)
    size = lax.axis_size("wide")
    placed = kernel_call(
        functools.partial(place_kernel, len(received)), [shape(received[0].shape)] * size,
        table, *received,
    )
    arrived = [swap(placed[2 * m + 1], "wide", 1) for m in range(1, size // 2)]
    terms = [placed[0], swap(placed[1], "wide", 1)]
    for m in range(1, size // 2):
        terms.append(swap(placed[2 * m] + arrived[m - 1], "wide", 2 * m))
    return terms


def update_kernel(terms, count, *refs):
    sums = refs[0][...]
    for term in refs[1:terms]:
        sums = sums + term[...]
    shifted_ref, dual_ref, penalty_ref, inverse_ref = refs[terms : terms + 4]
    outputs = refs[terms + 4 :]
    value_ref = outputs[-1]
    penalty = penalty_ref[:1, :1]
    inverse = inverse_ref[...]
    shifted, dual = shifted_ref[...], dual_ref[...]
    for _ in range(PASSES):
        target = jnp.dot(
            inverse, sums + penalty * shifted, precision=HIGHEST, preferred_element_type=jnp.float32
        )
        value = target - dual
        dual = jnp.maximum(-value, 0.0)
        shifted = jnp.abs(value)
    value_ref[...] = value
    height = outputs[0].shape[0]
    for d in range(count):
        outputs[d][...] = value_ref[rows_of(d, height), :]
    if len(outputs) > count + 1:
        store_pair(jnp.maximum(value, 0.0), outputs[count])


def admm(terms, shifted, dual, penalty, inverse, more):
    count = lax.axis_size("narrow")
    rank, width = shifted.shape
    out = [shape((rank // count, width))] * count
    if more:
        out += [shape((2 * rank, width), jnp.bfloat16)]
    return kernel_call(
        functools.partial(update_kernel, len(terms), count), out,
        *terms, shifted, dual, penalty, inverse,
        scratch=[pltpu.VMEM((rank, width), jnp.float32)],
        flops=12 * rank * rank * width * PASSES,
    )


def final_kernel(count, *refs):
    pieces, (factor_ref, dual_ref) = refs[:count], refs[count:]
    width = pieces[0].shape[1]

    def body(v):
        for d, piece in enumerate(pieces):
            lanes = slice((v ^ d) * width, ((v ^ d) + 1) * width)
            value = piece[...]
            factor_ref[:, lanes] = jnp.maximum(value, 0.0)
            dual_ref[:, lanes] = jnp.maximum(-value, 0.0)

    for_each_position(body)


def to_columns(pieces):
    received = swaps(pieces)
    height, width = received[0].shape
    count = len(received)
    factor, dual = kernel_call(
        functools.partial(final_kernel, count), [shape((height, count * width))] * 2,
        *received,
    )
    return factor.T, dual.T


def local(
    activity,
    tile_coords,
    user_owner,
    item_owner,
    user_factor,
    item_factor,
    time_factor,
    user_dual,
    item_dual,
):
    return sweep(
        activity, tile_coords, user_owner, item_owner, user_factor.T, item_factor.T,
        time_factor, user_dual.T, item_dual.T,
    )


def sweep(
    activity, tile_coords, user_owner, item_owner, user_factor, item_factor, time_factor,
    user_dual, item_dual,
):
    rank = time_factor.shape[1]
    count = lax.axis_size("narrow")
    user_table, item_table = positions(tile_coords, user_owner, item_owner)

    pieces = swaps(split(item_factor))
    rows = shape((rank, pieces[0].shape[1]))
    pair = shape((2 * rank, rows.shape[1]), jnp.bfloat16)
    item_rows, pair = kernel_call(functools.partial(pair_kernel, count), [rows, pair], *pieces)
    stack = jnp.concatenate([user_factor + user_dual, user_dual, item_dual])
    user_shifted, udual_rows, item_shifted, idual_rows = kernel_call(
        functools.partial(assemble_kernel, count), [rows] * 4,
        item_rows, *swaps(split(stack)),
    )

    pairs = all_pairs(pair)
    partials = tile_sums(activity, fetch_rows(pairs, item_table), time_factor, True)
    terms = owner_sums(partials, user_table)
    penalty, inverse = penalty_inverse(joint_gram(pairs), time_factor)
    *user_pieces, pair = admm(terms, user_shifted, udual_rows, penalty, inverse, True)

    pairs = all_pairs(pair)
    partials = tile_sums(activity, fetch_rows(pairs, user_table), time_factor, False)
    terms = owner_sums(partials, item_table)
    penalty, inverse = penalty_inverse(joint_gram(pairs), time_factor)
    new_users, new_user_dual = to_columns(user_pieces)
    item_pieces = admm(terms, item_shifted, idual_rows, penalty, inverse, False)
    new_items, new_item_dual = to_columns(item_pieces)
    return (new_users, new_items, new_user_dual, new_item_dual)


def solution(mesh):
    in_specs = (
        P(("wide", "narrow"), None, None, None),
        P(),
        P(),
        P(),
        P("wide", "narrow"),
        P("wide", "narrow"),
        P(),
        P("wide", "narrow"),
        P("wide", "narrow"),
    )
    out_specs = (P("wide", "narrow"), P("wide", "narrow"), P("wide", "narrow"), P("wide", "narrow"))
    return jax.shard_map(local, mesh=mesh, in_specs=in_specs, out_specs=out_specs, check_vma=False)
```

```python
import functools

import jax
import jax.numpy as jnp
from jax import lax
from jax.experimental import pallas as pl
from jax.experimental.pallas import tpu as pltpu
from jax.sharding import PartitionSpec as P


PASSES = 2
LEAF = 8
HIGHEST = lax.Precision.HIGHEST
ROOM = pltpu.CompilerParams(vmem_limit_bytes=16 * 2**20)


def eliminate(left, right):
    panel, width = left.shape
    lane = lax.broadcasted_iota(jnp.int32, (LEAF, width), 1)
    sub = lax.broadcasted_iota(jnp.int32, (LEAF, width), 0)
    for j in range(0, panel, LEAF):
        cols = [jnp.broadcast_to(left[:, j + m : j + m + 1], (panel, width)) for m in range(LEAF)]
        d = [c[j : j + LEAF] for c in cols]
        for k in range(LEAF):
            r = 1.0 / d[k][k : k + 1]
            pivot = d[k]
            here = sub == k
            for m in range(LEAF):
                if m != k:
                    f = d[m][k : k + 1] * r
                    d[m] = jnp.where(here, f, d[m] - pivot * f)
            d[k] = jnp.where(here, r, -pivot * r)
        inside = (lane >= j) & (lane < j + LEAF)
        el = jnp.where(inside, jnp.where(lane == sub + j, 1.0, 0.0), left[j : j + LEAF])
        er = right[j : j + LEAF]
        rl = sum(d[m] * el[m : m + 1] for m in range(LEAF))
        rr = sum(d[m] * er[m : m + 1] for m in range(LEAF))
        new_left, new_right = [], []
        for i in range(0, panel, LEAF):
            if i == j:
                new_left.append(rl)
                new_right.append(rr)
            else:
                c = [col[i : i + LEAF] for col in cols]
                ul = sum(c[m] * rl[m : m + 1] for m in range(LEAF))
                ur = sum(c[m] * rr[m : m + 1] for m in range(LEAF))
                new_left.append(jnp.where(inside, 0.0, left[i : i + LEAF]) - ul)
                new_right.append(right[i : i + LEAF] - ur)
        left = jnp.concatenate(new_left, 0)
        right = jnp.concatenate(new_right, 0)
    return left, right


def eliminate_panel(panel, k, work_ref):
    rank = work_ref.shape[0]
    half = rank // 2
    lane = lax.broadcasted_iota(jnp.int32, (1, rank), 1)
    rows = pl.ds(k * panel, panel)
    left, right = eliminate(work_ref[rows, :half], work_ref[rows, half:])
    done = jnp.concatenate([left, right], 1)
    full = work_ref[...]
    change = jnp.dot(full[:, :panel], done, precision=HIGHEST, preferred_element_type=jnp.float32)
    work_ref[...] = pltpu.roll(jnp.where(lane < panel, 0.0, full) - change, rank - panel, 1)
    work_ref[rows, :] = pltpu.roll(done, rank - panel, 1)


def first_half_kernel(panel, time_ref, *refs):
    pieces, (work_ref, penalty_ref) = refs[:-2], refs[-2:]
    rank = work_ref.shape[0]
    half = rank // 2
    for r, piece in enumerate(pieces):
        start = (lax.axis_index("wide") % 2 ^ r) * half
        work_ref[pl.ds(pl.multiple_of(start, half), half), :] = piece[...]
    time = time_ref[...]
    times = lax.dot_general(
        time, time, (((0,), (0,)), ((), ())), precision=HIGHEST, preferred_element_type=jnp.float32
    )
    gram = work_ref[...] * times
    row = lax.broadcasted_iota(jnp.int32, (rank, rank), 0)
    col = lax.broadcasted_iota(jnp.int32, (rank, rank), 1)
    trace = jnp.sum(jnp.where(row == col, gram, 0.0), axis=0, keepdims=True)
    penalty = jnp.sum(trace, axis=1, keepdims=True) / rank
    penalty_ref[...] = jnp.broadcast_to(penalty, penalty_ref.shape)
    work_ref[...] = gram + jnp.where(row == col, penalty, 0.0)
    eliminate_panel(panel, 0, work_ref)


def second_half_kernel(panel, half_ref, inverse_ref):
    inverse_ref[...] = half_ref[...]
    eliminate_panel(panel, 1, inverse_ref)


def penalty_inverse(pieces, time_factor):
    rank = time_factor.shape[1]
    half, penalty = kernel_call(
        functools.partial(first_half_kernel, rank // 2),
        [shape((rank, rank)), shape((1, 128))], time_factor, *pieces, flops=6_000_000_000,
    )
    (inverse,) = kernel_call(
        functools.partial(second_half_kernel, rank // 2),
        [shape((rank, rank))], half, flops=6_000_000_000,
    )
    return penalty, inverse


def kernel_call(kernel, out_shape, *args, scratch=(), flops=1_000_000, smem=False):
    spec = pl.BlockSpec(memory_space=pltpu.SMEM) if smem else pl.BlockSpec(memory_space=pltpu.VMEM)
    size = sum(x.size * x.dtype.itemsize for x in (*args, *out_shape))
    return pl.pallas_call(
        kernel,
        out_shape=tuple(out_shape),
        in_specs=[spec] * len(args),
        out_specs=tuple(pl.BlockSpec(memory_space=pltpu.VMEM) for _ in out_shape),
        scratch_shapes=list(scratch),
        compiler_params=ROOM,
        cost_estimate=pl.CostEstimate(flops=flops, bytes_accessed=size, transcendentals=0),
    )(*args)


def shape(dims, dtype=jnp.float32):
    return jax.ShapeDtypeStruct(tuple(dims), dtype)


def swap(x, axis, mask):
    size = lax.axis_size(axis)
    return lax.ppermute(x, axis, [(i, i ^ mask) for i in range(size)])


def swaps(pieces):
    received = list(pieces)
    for d in reversed(range(1, len(pieces))):
        received[d] = swap(pieces[d], "narrow", d)
    return received


def for_each_position(body):
    me = lax.axis_index("narrow")
    for v in range(lax.axis_size("narrow")):
        pl.when(me == v)(functools.partial(body, v))


def rows_of(d, height):
    return pl.ds(pl.multiple_of((lax.axis_index("narrow") ^ d) * height, height), height)


def positions_kernel(coords_ref, user_ref, item_ref, table_ref):
    wide, narrow = lax.axis_index("wide"), lax.axis_index("narrow")
    count = lax.axis_size("narrow")
    for d in range(count):
        tile = wide * count + (narrow ^ d)
        user = user_ref[coords_ref[0, tile]] ^ wide
        item = item_ref[coords_ref[1, tile]] ^ wide
        table_ref[d : d + 1, :] = jnp.full((1, 128), user, jnp.int32)
        table_ref[count + d : count + d + 1, :] = jnp.full((1, 128), item, jnp.int32)


def positions(tile_coords, user_owner, item_owner):
    count = lax.axis_size("narrow")
    (table,) = kernel_call(
        positions_kernel, [shape((2 * count, 128), jnp.int32)],
        tile_coords.T, user_owner, item_owner, smem=True,
    )
    return table[:count], table[count:]


def split_kernel(stack_ref, *outputs):
    width = outputs[0].shape[1]

    def body(v):
        for d, out in enumerate(outputs):
            out[...] = stack_ref[:, (v ^ d) * width : ((v ^ d) + 1) * width]

    for_each_position(body)


def split(stack):
    count = lax.axis_size("narrow")
    height, rows = stack.shape
    return kernel_call(split_kernel, [shape((height, rows // count))] * count, stack)


def store_pair(value, pair_ref):
    rank = value.shape[0]
    rounded = value.astype(pair_ref.dtype)
    pair_ref[:rank] = rounded
    pair_ref[rank:] = (value - rounded.astype(jnp.float32)).astype(pair_ref.dtype)


def pair_kernel(count, *refs):
    pieces, (factor_ref, pair_ref) = refs[:count], refs[count:]
    height = pieces[0].shape[0]
    for d, piece in enumerate(pieces):
        factor_ref[rows_of(d, height), :] = piece[...]
    store_pair(factor_ref[...], pair_ref)


def assemble_kernel(count, *refs):
    factor_ref, pieces, outputs = refs[0], refs[1 : count + 1], refs[count + 1 :]
    height = pieces[0].shape[0] // 3
    for d, piece in enumerate(pieces):
        rows = rows_of(d, height)
        outputs[0][rows, :] = piece[:height] + piece[height : 2 * height]
        outputs[1][rows, :] = piece[height : 2 * height]
        outputs[3][rows, :] = piece[2 * height :]
    outputs[2][...] = factor_ref[...] + outputs[3][...]


def gram_kernel(*refs):
    pairs, (half_ref, rows_ref) = refs[:-2], refs[-2:]
    rank = rows_ref.shape[0]
    width = pairs[0].shape[1]
    for k, pair in enumerate(pairs):
        rows_ref[:, k * width : (k + 1) * width] = pair[:rank].astype(jnp.float32) + pair[
            rank:
        ].astype(jnp.float32)
    half = half_ref.shape[0]
    start = pl.multiple_of(lax.axis_index("wide") % 2 * half, half)
    half_ref[...] = lax.dot_general(
        rows_ref[pl.ds(start, half), :], rows_ref[...], (((1,), (1,)), ((), ())),
        precision=HIGHEST, preferred_element_type=jnp.float32,
    )


def joint_gram(pairs):
    rank, width = pairs[0].shape[0] // 2, pairs[0].shape[1]
    (total,) = kernel_call(
        gram_kernel, [shape((rank // 2, rank))], *pairs,
        scratch=[pltpu.VMEM((rank, len(pairs) * width), jnp.float32)],
        flops=1_500_000_000,
    )
    mask = 1
    while mask < lax.axis_size("narrow"):
        total = total + swap(total, "narrow", mask)
        mask *= 2
    return total, swap(total, "wide", 1)


def pick_kernel(count, table_ref, *refs):
    pairs, outputs = refs[:-count], refs[-count:]
    for d, out in enumerate(outputs):
        rank = out.shape[0]
        here = table_ref[d : d + 1, :1].astype(jnp.float32).astype(out.dtype)
        here = jnp.broadcast_to(here, out.shape)
        value = pairs[0][:rank]
        for r in range(1, len(pairs)):
            value = jnp.where(here == r, pairs[r][:rank], value)
        out[...] = value


def all_pairs(pair):
    chips = lax.axis_size("wide") // 2
    same = [pair] * chips
    for m in reversed(range(1, chips)):
        same[m] = swap(pair, "wide", 2 * m)
    return [x for a in same for x in (a, swap(a, "wide", 1))]


def fetch_rows(pairs, table):
    count = lax.axis_size("narrow")
    rank, width = pairs[0].shape[0] // 2, pairs[0].shape[1]
    picked = kernel_call(
        functools.partial(pick_kernel, count), [shape((rank, width), jnp.bfloat16)] * count,
        table, *pairs, flops=5_000_000_000,
    )
    return swaps(picked)


def tile_kernel(forward, count, activity_ref, time_ref, *refs):
    pieces, outputs, (stage_ref, sums_ref) = refs[:count], refs[count : 2 * count], refs[2 * count :]
    me = lax.axis_index("narrow")
    for d, piece in enumerate(pieces):
        stage_ref[me ^ d] = piece[...]
    low = jnp.concatenate([stage_ref[q] for q in range(count)], axis=1)
    low = low.astype(jnp.float32)
    times = time_ref[...].T
    total = None
    for k in range(activity_ref.shape[1]):
        khatri = (low * times[:, k : k + 1]).astype(jnp.bfloat16)
        dims = (((1,), (1 if forward else 0,)), ((), ()))
        term = lax.dot_general(khatri, activity_ref[0, k], dims, preferred_element_type=jnp.float32)
        total = term if total is None else total + term
    width = outputs[0].shape[1]
    for q in range(count):
        sums_ref[q] = total[:, q * width : (q + 1) * width]
    for d, out in enumerate(outputs):
        out[...] = sums_ref[me ^ d]


def tile_sums(activity, pieces, time_factor, forward):
    count = len(pieces)
    rank = time_factor.shape[1]
    _, steps, rows, cols = activity.shape
    width = (rows if forward else cols) // count
    return kernel_call(
        functools.partial(tile_kernel, forward, count), [shape((rank, width))] * count,
        activity, time_factor, *pieces,
        scratch=[
            pltpu.VMEM((count, *pieces[0].shape), jnp.bfloat16),
            pltpu.VMEM((count, rank, width), jnp.float32),
        ],
        flops=2 * rank * steps * rows * cols,
    )


def place_kernel(count, table_ref, *refs):
    received, outputs = refs[:count], refs[count:]
    values = [x[...] for x in received]
    for r, out in enumerate(outputs):
        total = None
        for d, value in enumerate(values):
            here = jnp.broadcast_to(table_ref[d : d + 1, :1] == r, value.shape)
            term = jnp.where(here, value, 0.0)
            total = term if total is None else total + term
        out[...] = total


def owner_sums(partials, table):
    received = swaps(partials)
    size = lax.axis_size("wide")
    placed = kernel_call(
        functools.partial(place_kernel, len(received)), [shape(received[0].shape)] * size,
        table, *received,
    )
    order = [*reversed(range(1, size // 2)), 0]
    arrived = {m: swap(placed[2 * m + 1], "wide", 1) for m in order}
    terms = [placed[0], arrived[0]]
    for m in order[:-1]:
        terms.append(swap(placed[2 * m] + arrived[m], "wide", 2 * m))
    return terms


def update_kernel(terms, count, *refs):
    sums = refs[0][...]
    for term in refs[1:terms]:
        sums = sums + term[...]
    shifted_ref, dual_ref, penalty_ref, inverse_ref = refs[terms : terms + 4]
    outputs = refs[terms + 4 :]
    value_ref = outputs[-1]
    penalty = penalty_ref[:1, :1]
    inverse = inverse_ref[...]
    shifted, dual = shifted_ref[...], dual_ref[...]
    for _ in range(PASSES):
        target = jnp.dot(
            inverse, sums + penalty * shifted, precision=HIGHEST, preferred_element_type=jnp.float32
        )
        value = target - dual
        dual = jnp.maximum(-value, 0.0)
        shifted = jnp.abs(value)
    value_ref[...] = value
    height = outputs[0].shape[0]
    for d in range(count):
        outputs[d][...] = value_ref[rows_of(d, height), :]
    if len(outputs) > count + 1:
        store_pair(jnp.maximum(value, 0.0), outputs[count])


def admm(terms, shifted, dual, penalty, inverse, more):
    count = lax.axis_size("narrow")
    rank, width = shifted.shape
    out = [shape((rank // count, width))] * count
    if more:
        out += [shape((2 * rank, width), jnp.bfloat16)]
    return kernel_call(
        functools.partial(update_kernel, len(terms), count), out,
        *terms, shifted, dual, penalty, inverse,
        scratch=[pltpu.VMEM((rank, width), jnp.float32)],
        flops=12 * rank * rank * width * PASSES,
    )


def final_kernel(count, *refs):
    pieces, (factor_ref, dual_ref) = refs[:count], refs[count:]
    width = pieces[0].shape[1]

    def body(v):
        for d, piece in enumerate(pieces):
            lanes = slice((v ^ d) * width, ((v ^ d) + 1) * width)
            value = piece[...]
            factor_ref[:, lanes] = jnp.maximum(value, 0.0)
            dual_ref[:, lanes] = jnp.maximum(-value, 0.0)

    for_each_position(body)


def to_columns(pieces):
    received = swaps(pieces)
    height, width = received[0].shape
    count = len(received)
    factor, dual = kernel_call(
        functools.partial(final_kernel, count), [shape((height, count * width))] * 2,
        *received,
    )
    return factor.T, dual.T


def local(
    activity,
    tile_coords,
    user_owner,
    item_owner,
    user_factor,
    item_factor,
    time_factor,
    user_dual,
    item_dual,
):
    return sweep(
        activity, tile_coords, user_owner, item_owner, user_factor.T, item_factor.T,
        time_factor, user_dual.T, item_dual.T,
    )


def sweep(
    activity, tile_coords, user_owner, item_owner, user_factor, item_factor, time_factor,
    user_dual, item_dual,
):
    rank = time_factor.shape[1]
    count = lax.axis_size("narrow")
    user_table, item_table = positions(tile_coords, user_owner, item_owner)

    pieces = swaps(split(item_factor))
    rows = shape((rank, pieces[0].shape[1]))
    pair = shape((2 * rank, rows.shape[1]), jnp.bfloat16)
    item_rows, pair = kernel_call(functools.partial(pair_kernel, count), [rows, pair], *pieces)
    stack = jnp.concatenate([user_factor, user_dual, item_dual])
    user_shifted, udual_rows, item_shifted, idual_rows = kernel_call(
        functools.partial(assemble_kernel, count), [rows] * 4,
        item_rows, *swaps(split(stack)),
    )

    pairs = all_pairs(pair)
    partials = tile_sums(activity, fetch_rows(pairs, item_table), time_factor, True)
    terms = owner_sums(partials, user_table)
    penalty, inverse = penalty_inverse(joint_gram(pairs), time_factor)
    *user_pieces, pair = admm(terms, user_shifted, udual_rows, penalty, inverse, True)

    pairs = all_pairs(pair)
    partials = tile_sums(activity, fetch_rows(pairs, user_table), time_factor, False)
    terms = owner_sums(partials, item_table)
    penalty, inverse = penalty_inverse(joint_gram(pairs), time_factor)
    new_users, new_user_dual = to_columns(user_pieces)
    item_pieces = admm(terms, item_shifted, idual_rows, penalty, inverse, False)
    new_items, new_item_dual = to_columns(item_pieces)
    return (new_users, new_items, new_user_dual, new_item_dual)


def solution(mesh):
    in_specs = (
        P(("wide", "narrow"), None, None, None),
        P(),
        P(),
        P(),
        P("wide", "narrow"),
        P("wide", "narrow"),
        P(),
        P("wide", "narrow"),
        P("wide", "narrow"),
    )
    out_specs = (P("wide", "narrow"), P("wide", "narrow"), P("wide", "narrow"), P("wide", "narrow"))
    return jax.shard_map(local, mesh=mesh, in_specs=in_specs, out_specs=out_specs, check_vma=False)
```

```python
import functools

import jax
import jax.numpy as jnp
from jax import lax
from jax.experimental import pallas as pl
from jax.experimental.pallas import tpu as pltpu
from jax.sharding import PartitionSpec as P


PASSES = 2
LEAF = 8
HIGHEST = lax.Precision.HIGHEST
ROOM = pltpu.CompilerParams(vmem_limit_bytes=16 * 2**20)


def eliminate(left, right):
    panel, width = left.shape
    lane = lax.broadcasted_iota(jnp.int32, (LEAF, width), 1)
    sub = lax.broadcasted_iota(jnp.int32, (LEAF, width), 0)
    for j in range(0, panel, LEAF):
        cols = [jnp.broadcast_to(left[:, j + m : j + m + 1], (panel, width)) for m in range(LEAF)]
        d = [c[j : j + LEAF] for c in cols]
        for k in range(LEAF):
            r = 1.0 / d[k][k : k + 1]
            pivot = d[k]
            here = sub == k
            for m in range(LEAF):
                if m != k:
                    f = d[m][k : k + 1] * r
                    d[m] = jnp.where(here, f, d[m] - pivot * f)
            d[k] = jnp.where(here, r, -pivot * r)
        inside = (lane >= j) & (lane < j + LEAF)
        el = jnp.where(inside, jnp.where(lane == sub + j, 1.0, 0.0), left[j : j + LEAF])
        er = right[j : j + LEAF]
        rl = sum(d[m] * el[m : m + 1] for m in range(LEAF))
        rr = sum(d[m] * er[m : m + 1] for m in range(LEAF))
        new_left, new_right = [], []
        for i in range(0, panel, LEAF):
            if i == j:
                new_left.append(rl)
                new_right.append(rr)
            else:
                c = [col[i : i + LEAF] for col in cols]
                ul = sum(c[m] * rl[m : m + 1] for m in range(LEAF))
                ur = sum(c[m] * rr[m : m + 1] for m in range(LEAF))
                new_left.append(jnp.where(inside, 0.0, left[i : i + LEAF]) - ul)
                new_right.append(right[i : i + LEAF] - ur)
        left = jnp.concatenate(new_left, 0)
        right = jnp.concatenate(new_right, 0)
    return left, right


def eliminate_panel(panel, k, work_ref):
    rank = work_ref.shape[0]
    half = rank // 2
    lane = lax.broadcasted_iota(jnp.int32, (1, rank), 1)
    rows = pl.ds(k * panel, panel)
    left, right = eliminate(work_ref[rows, :half], work_ref[rows, half:])
    done = jnp.concatenate([left, right], 1)
    full = work_ref[...]
    change = jnp.dot(full[:, :panel], done, precision=HIGHEST, preferred_element_type=jnp.float32)
    work_ref[...] = pltpu.roll(jnp.where(lane < panel, 0.0, full) - change, rank - panel, 1)
    work_ref[rows, :] = pltpu.roll(done, rank - panel, 1)


def first_half_kernel(panel, time_ref, *refs):
    pieces, (work_ref, penalty_ref) = refs[:-2], refs[-2:]
    rank = work_ref.shape[0]
    part = rank // 4
    for r, piece in enumerate(pieces):
        core = lax.axis_index("wide") % 2 ^ r % 2
        side = lax.axis_index("narrow") % 2 ^ r // 2
        start = pl.multiple_of((core * 2 + side) * part, part)
        work_ref[pl.ds(start, part), :] = piece[...]
    time = time_ref[...]
    times = lax.dot_general(
        time, time, (((0,), (0,)), ((), ())), precision=HIGHEST, preferred_element_type=jnp.float32
    )
    gram = work_ref[...] * times
    row = lax.broadcasted_iota(jnp.int32, (rank, rank), 0)
    col = lax.broadcasted_iota(jnp.int32, (rank, rank), 1)
    trace = jnp.sum(jnp.where(row == col, gram, 0.0), axis=0, keepdims=True)
    penalty = jnp.sum(trace, axis=1, keepdims=True) / rank
    penalty_ref[...] = jnp.broadcast_to(penalty, penalty_ref.shape)
    work_ref[...] = gram + jnp.where(row == col, penalty, 0.0)
    eliminate_panel(panel, 0, work_ref)


def second_half_kernel(panel, half_ref, inverse_ref):
    inverse_ref[...] = half_ref[...]
    eliminate_panel(panel, 1, inverse_ref)


def penalty_inverse(pieces, time_factor):
    rank = time_factor.shape[1]
    half, penalty = kernel_call(
        functools.partial(first_half_kernel, rank // 2),
        [shape((rank, rank)), shape((1, 128))], time_factor, *pieces, flops=6_000_000_000,
    )
    (inverse,) = kernel_call(
        functools.partial(second_half_kernel, rank // 2),
        [shape((rank, rank))], half, flops=6_000_000_000,
    )
    return penalty, inverse


def kernel_call(kernel, out_shape, *args, scratch=(), flops=1_000_000, smem=False):
    spec = pl.BlockSpec(memory_space=pltpu.SMEM) if smem else pl.BlockSpec(memory_space=pltpu.VMEM)
    size = sum(x.size * x.dtype.itemsize for x in (*args, *out_shape))
    return pl.pallas_call(
        kernel,
        out_shape=tuple(out_shape),
        in_specs=[spec] * len(args),
        out_specs=tuple(pl.BlockSpec(memory_space=pltpu.VMEM) for _ in out_shape),
        scratch_shapes=list(scratch),
        compiler_params=ROOM,
        cost_estimate=pl.CostEstimate(flops=flops, bytes_accessed=size, transcendentals=0),
    )(*args)


def shape(dims, dtype=jnp.float32):
    return jax.ShapeDtypeStruct(tuple(dims), dtype)


def swap(x, axis, mask):
    size = lax.axis_size(axis)
    return lax.ppermute(x, axis, [(i, i ^ mask) for i in range(size)])


def swaps(pieces):
    received = list(pieces)
    for d in reversed(range(1, len(pieces))):
        received[d] = swap(pieces[d], "narrow", d)
    return received


def for_each_position(body):
    me = lax.axis_index("narrow")
    for v in range(lax.axis_size("narrow")):
        pl.when(me == v)(functools.partial(body, v))


def rows_of(d, height):
    return pl.ds(pl.multiple_of((lax.axis_index("narrow") ^ d) * height, height), height)


def positions_kernel(coords_ref, user_ref, item_ref, table_ref):
    wide, narrow = lax.axis_index("wide"), lax.axis_index("narrow")
    count = lax.axis_size("narrow")
    for d in range(count):
        tile = wide * count + (narrow ^ d)
        user = user_ref[coords_ref[0, tile]] ^ wide
        item = item_ref[coords_ref[1, tile]] ^ wide
        table_ref[d : d + 1, :] = jnp.full((1, 128), user, jnp.int32)
        table_ref[count + d : count + d + 1, :] = jnp.full((1, 128), item, jnp.int32)


def positions(tile_coords, user_owner, item_owner):
    count = lax.axis_size("narrow")
    (table,) = kernel_call(
        positions_kernel, [shape((2 * count, 128), jnp.int32)],
        tile_coords.T, user_owner, item_owner, smem=True,
    )
    return table[:count], table[count:]


def split_kernel(stack_ref, *outputs):
    width = outputs[0].shape[1]

    def body(v):
        for d, out in enumerate(outputs):
            out[...] = stack_ref[:, (v ^ d) * width : ((v ^ d) + 1) * width]

    for_each_position(body)


def split(stack):
    count = lax.axis_size("narrow")
    height, rows = stack.shape
    return kernel_call(split_kernel, [shape((height, rows // count))] * count, stack)


def store_pair(value, pair_ref):
    rank = value.shape[0]
    rounded = value.astype(pair_ref.dtype)
    pair_ref[:rank] = rounded
    pair_ref[rank:] = (value - rounded.astype(jnp.float32)).astype(pair_ref.dtype)


def pair_kernel(count, *refs):
    pieces, (factor_ref, pair_ref) = refs[:count], refs[count:]
    height = pieces[0].shape[0]
    for d, piece in enumerate(pieces):
        factor_ref[rows_of(d, height), :] = piece[...]
    store_pair(factor_ref[...], pair_ref)


def assemble_kernel(count, *refs):
    factor_ref, pieces, outputs = refs[0], refs[1 : count + 1], refs[count + 1 :]
    height = pieces[0].shape[0] // 3
    for d, piece in enumerate(pieces):
        rows = rows_of(d, height)
        outputs[0][rows, :] = piece[:height] + piece[height : 2 * height]
        outputs[1][rows, :] = piece[height : 2 * height]
        outputs[3][rows, :] = piece[2 * height :]
    outputs[2][...] = factor_ref[...] + outputs[3][...]


def gram_kernel(*refs):
    pairs, (far_ref, near_ref, rows_ref, half_ref) = refs[:-4], refs[-4:]
    rank = rows_ref.shape[0]
    width = pairs[0].shape[1]
    for k, pair in enumerate(pairs):
        rows_ref[:, k * width : (k + 1) * width] = pair[:rank].astype(jnp.float32) + pair[
            rank:
        ].astype(jnp.float32)
    half, part = half_ref.shape[0], near_ref.shape[0]
    start = pl.multiple_of(lax.axis_index("wide") % 2 * half, half)
    half_ref[...] = lax.dot_general(
        rows_ref[pl.ds(start, half), :], rows_ref[...], (((1,), (1,)), ((), ())),
        precision=HIGHEST, preferred_element_type=jnp.float32,
    )
    side = lax.axis_index("narrow") % 2
    near_ref[...] = half_ref[pl.ds(pl.multiple_of(side * part, part), part), :]
    far_ref[...] = half_ref[pl.ds(pl.multiple_of((1 - side) * part, part), part), :]


def joint_gram(pairs):
    rank, width = pairs[0].shape[0] // 2, pairs[0].shape[1]
    far, near = kernel_call(
        gram_kernel, [shape((rank // 4, rank))] * 2, *pairs,
        scratch=[
            pltpu.VMEM((rank, len(pairs) * width), jnp.float32),
            pltpu.VMEM((rank // 2, rank), jnp.float32),
        ],
        flops=1_500_000_000,
    )
    total = near + swap(far, "narrow", 1)
    mask = 2
    while mask < lax.axis_size("narrow"):
        total = total + swap(total, "narrow", mask)
        mask *= 2
    parts = [total, swap(total, "narrow", 1)]
    return [x for part in parts for x in (part, swap(part, "wide", 1))]


def pick_kernel(count, table_ref, *refs):
    pairs, outputs = refs[:-count], refs[-count:]
    for d, out in enumerate(outputs):
        rank = out.shape[0]
        here = table_ref[d : d + 1, :1].astype(jnp.float32).astype(out.dtype)
        here = jnp.broadcast_to(here, out.shape)
        value = pairs[0][:rank]
        for r in range(1, len(pairs)):
            value = jnp.where(here == r, pairs[r][:rank], value)
        out[...] = value


def all_pairs(pair):
    chips = lax.axis_size("wide") // 2
    same = [pair] * chips
    for m in reversed(range(1, chips)):
        same[m] = swap(pair, "wide", 2 * m)
    return [x for a in same for x in (a, swap(a, "wide", 1))]


def fetch_rows(pairs, table):
    count = lax.axis_size("narrow")
    rank, width = pairs[0].shape[0] // 2, pairs[0].shape[1]
    picked = kernel_call(
        functools.partial(pick_kernel, count), [shape((rank, width), jnp.bfloat16)] * count,
        table, *pairs, flops=5_000_000_000,
    )
    return swaps(picked)


def tile_kernel(forward, count, activity_ref, time_ref, *refs):
    pieces, outputs, (stage_ref, sums_ref) = refs[:count], refs[count : 2 * count], refs[2 * count :]
    me = lax.axis_index("narrow")
    for d, piece in enumerate(pieces):
        stage_ref[me ^ d] = piece[...]
    low = jnp.concatenate([stage_ref[q] for q in range(count)], axis=1)
    low = low.astype(jnp.float32)
    times = time_ref[...].T
    total = None
    for k in range(activity_ref.shape[1]):
        khatri = (low * times[:, k : k + 1]).astype(jnp.bfloat16)
        dims = (((1,), (1 if forward else 0,)), ((), ()))
        term = lax.dot_general(khatri, activity_ref[0, k], dims, preferred_element_type=jnp.float32)
        total = term if total is None else total + term
    width = outputs[0].shape[1]
    for q in range(count):
        sums_ref[q] = total[:, q * width : (q + 1) * width]
    for d, out in enumerate(outputs):
        out[...] = sums_ref[me ^ d]


def tile_sums(activity, pieces, time_factor, forward):
    count = len(pieces)
    rank = time_factor.shape[1]
    _, steps, rows, cols = activity.shape
    width = (rows if forward else cols) // count
    return kernel_call(
        functools.partial(tile_kernel, forward, count), [shape((rank, width))] * count,
        activity, time_factor, *pieces,
        scratch=[
            pltpu.VMEM((count, *pieces[0].shape), jnp.bfloat16),
            pltpu.VMEM((count, rank, width), jnp.float32),
        ],
        flops=2 * rank * steps * rows * cols,
    )


def place_kernel(count, table_ref, *refs):
    received, outputs = refs[:count], refs[count:]
    values = [x[...] for x in received]
    for r, out in enumerate(outputs):
        total = None
        for d, value in enumerate(values):
            here = jnp.broadcast_to(table_ref[d : d + 1, :1] == r, value.shape)
            term = jnp.where(here, value, 0.0)
            total = term if total is None else total + term
        out[...] = total


def owner_sums(partials, table):
    received = swaps(partials)
    size = lax.axis_size("wide")
    placed = kernel_call(
        functools.partial(place_kernel, len(received)), [shape(received[0].shape)] * size,
        table, *received,
    )
    order = [*reversed(range(1, size // 2)), 0]
    arrived = {m: swap(placed[2 * m + 1], "wide", 1) for m in order}
    terms = [placed[0], arrived[0]]
    for m in order[:-1]:
        terms.append(swap(placed[2 * m] + arrived[m], "wide", 2 * m))
    return terms


def update_kernel(terms, count, *refs):
    sums = refs[0][...]
    for term in refs[1:terms]:
        sums = sums + term[...]
    shifted_ref, dual_ref, penalty_ref, inverse_ref = refs[terms : terms + 4]
    outputs = refs[terms + 4 :]
    value_ref = outputs[-1]
    penalty = penalty_ref[:1, :1]
    inverse = inverse_ref[...]
    shifted, dual = shifted_ref[...], dual_ref[...]
    for _ in range(PASSES):
        target = jnp.dot(
            inverse, sums + penalty * shifted, precision=HIGHEST, preferred_element_type=jnp.float32
        )
        value = target - dual
        dual = jnp.maximum(-value, 0.0)
        shifted = jnp.abs(value)
    value_ref[...] = value
    height = outputs[0].shape[0]
    for d in range(count):
        outputs[d][...] = value_ref[rows_of(d, height), :]
    if len(outputs) > count + 1:
        store_pair(jnp.maximum(value, 0.0), outputs[count])


def admm(terms, shifted, dual, penalty, inverse, more):
    count = lax.axis_size("narrow")
    rank, width = shifted.shape
    out = [shape((rank // count, width))] * count
    if more:
        out += [shape((2 * rank, width), jnp.bfloat16)]
    return kernel_call(
        functools.partial(update_kernel, len(terms), count), out,
        *terms, shifted, dual, penalty, inverse,
        scratch=[pltpu.VMEM((rank, width), jnp.float32)],
        flops=12 * rank * rank * width * PASSES,
    )


def final_kernel(count, *refs):
    pieces, (factor_ref, dual_ref) = refs[:count], refs[count:]
    width = pieces[0].shape[1]

    def body(v):
        for d, piece in enumerate(pieces):
            lanes = slice((v ^ d) * width, ((v ^ d) + 1) * width)
            value = piece[...]
            factor_ref[:, lanes] = jnp.maximum(value, 0.0)
            dual_ref[:, lanes] = jnp.maximum(-value, 0.0)

    for_each_position(body)


def to_columns(pieces):
    received = swaps(pieces)
    height, width = received[0].shape
    count = len(received)
    factor, dual = kernel_call(
        functools.partial(final_kernel, count), [shape((height, count * width))] * 2,
        *received,
    )
    return factor.T, dual.T


def local(
    activity,
    tile_coords,
    user_owner,
    item_owner,
    user_factor,
    item_factor,
    time_factor,
    user_dual,
    item_dual,
):
    return sweep(
        activity, tile_coords, user_owner, item_owner, user_factor.T, item_factor.T,
        time_factor, user_dual.T, item_dual.T,
    )


def sweep(
    activity, tile_coords, user_owner, item_owner, user_factor, item_factor, time_factor,
    user_dual, item_dual,
):
    rank = time_factor.shape[1]
    count = lax.axis_size("narrow")
    user_table, item_table = positions(tile_coords, user_owner, item_owner)

    pieces = swaps(split(item_factor))
    rows = shape((rank, pieces[0].shape[1]))
    pair = shape((2 * rank, rows.shape[1]), jnp.bfloat16)
    item_rows, pair = kernel_call(functools.partial(pair_kernel, count), [rows, pair], *pieces)
    stack = jnp.concatenate([user_factor, user_dual, item_dual])
    user_shifted, udual_rows, item_shifted, idual_rows = kernel_call(
        functools.partial(assemble_kernel, count), [rows] * 4,
        item_rows, *swaps(split(stack)),
    )

    pairs = all_pairs(pair)
    partials = tile_sums(activity, fetch_rows(pairs, item_table), time_factor, True)
    terms = owner_sums(partials, user_table)
    penalty, inverse = penalty_inverse(joint_gram(pairs), time_factor)
    *user_pieces, pair = admm(terms, user_shifted, udual_rows, penalty, inverse, True)

    pairs = all_pairs(pair)
    partials = tile_sums(activity, fetch_rows(pairs, user_table), time_factor, False)
    terms = owner_sums(partials, item_table)
    penalty, inverse = penalty_inverse(joint_gram(pairs), time_factor)
    new_users, new_user_dual = to_columns(user_pieces)
    item_pieces = admm(terms, item_shifted, idual_rows, penalty, inverse, False)
    new_items, new_item_dual = to_columns(item_pieces)
    return (new_users, new_items, new_user_dual, new_item_dual)


def solution(mesh):
    in_specs = (
        P(("wide", "narrow"), None, None, None),
        P(),
        P(),
        P(),
        P("wide", "narrow"),
        P("wide", "narrow"),
        P(),
        P("wide", "narrow"),
        P("wide", "narrow"),
    )
    out_specs = (P("wide", "narrow"), P("wide", "narrow"), P("wide", "narrow"), P("wide", "narrow"))
    return jax.shard_map(local, mesh=mesh, in_specs=in_specs, out_specs=out_specs, check_vma=False)
```

```python
import functools

import jax
import jax.numpy as jnp
from jax import lax
from jax.experimental import pallas as pl
from jax.experimental.pallas import tpu as pltpu
from jax.sharding import PartitionSpec as P


PASSES = 2
LEAF = 8
HIGHEST = lax.Precision.HIGHEST
ROOM = pltpu.CompilerParams(vmem_limit_bytes=16 * 2**20)


def eliminate(left, right):
    panel, width = left.shape
    lane = lax.broadcasted_iota(jnp.int32, (LEAF, width), 1)
    sub = lax.broadcasted_iota(jnp.int32, (LEAF, width), 0)
    for j in range(0, panel, LEAF):
        cols = [jnp.broadcast_to(left[:, j + m : j + m + 1], (panel, width)) for m in range(LEAF)]
        d = [c[j : j + LEAF] for c in cols]
        for k in range(LEAF):
            r = 1.0 / d[k][k : k + 1]
            pivot = d[k]
            here = sub == k
            for m in range(LEAF):
                if m != k:
                    f = d[m][k : k + 1] * r
                    d[m] = jnp.where(here, f, d[m] - pivot * f)
            d[k] = jnp.where(here, r, -pivot * r)
        inside = (lane >= j) & (lane < j + LEAF)
        el = jnp.where(inside, jnp.where(lane == sub + j, 1.0, 0.0), left[j : j + LEAF])
        er = right[j : j + LEAF]
        rl = sum(d[m] * el[m : m + 1] for m in range(LEAF))
        rr = sum(d[m] * er[m : m + 1] for m in range(LEAF))
        new_left, new_right = [], []
        for i in range(0, panel, LEAF):
            if i == j:
                new_left.append(rl)
                new_right.append(rr)
            else:
                c = [col[i : i + LEAF] for col in cols]
                ul = sum(c[m] * rl[m : m + 1] for m in range(LEAF))
                ur = sum(c[m] * rr[m : m + 1] for m in range(LEAF))
                new_left.append(jnp.where(inside, 0.0, left[i : i + LEAF]) - ul)
                new_right.append(right[i : i + LEAF] - ur)
        left = jnp.concatenate(new_left, 0)
        right = jnp.concatenate(new_right, 0)
    return left, right


def eliminate_panel(panel, k, work_ref):
    rank = work_ref.shape[0]
    half = rank // 2
    lane = lax.broadcasted_iota(jnp.int32, (1, rank), 1)
    rows = pl.ds(k * panel, panel)
    left, right = eliminate(work_ref[rows, :half], work_ref[rows, half:])
    done = jnp.concatenate([left, right], 1)
    full = work_ref[...]
    change = jnp.dot(full[:, :panel], done, precision=HIGHEST, preferred_element_type=jnp.float32)
    work_ref[...] = pltpu.roll(jnp.where(lane < panel, 0.0, full) - change, rank - panel, 1)
    work_ref[rows, :] = pltpu.roll(done, rank - panel, 1)


def first_half_kernel(panel, time_ref, *refs):
    pieces, (work_ref, penalty_ref) = refs[:-2], refs[-2:]
    rank = work_ref.shape[0]
    half = rank // 2
    for r, piece in enumerate(pieces):
        start = (lax.axis_index("wide") % 2 ^ r) * half
        work_ref[pl.ds(pl.multiple_of(start, half), half), :] = piece[...]
    time = time_ref[...]
    times = lax.dot_general(
        time, time, (((0,), (0,)), ((), ())), precision=HIGHEST, preferred_element_type=jnp.float32
    )
    gram = work_ref[...] * times
    row = lax.broadcasted_iota(jnp.int32, (rank, rank), 0)
    col = lax.broadcasted_iota(jnp.int32, (rank, rank), 1)
    trace = jnp.sum(jnp.where(row == col, gram, 0.0), axis=0, keepdims=True)
    penalty = jnp.sum(trace, axis=1, keepdims=True) / rank
    penalty_ref[...] = jnp.broadcast_to(penalty, penalty_ref.shape)
    work_ref[...] = gram + jnp.where(row == col, penalty, 0.0)
    eliminate_panel(panel, 0, work_ref)


def second_half_kernel(panel, half_ref, inverse_ref):
    inverse_ref[...] = half_ref[...]
    eliminate_panel(panel, 1, inverse_ref)


def penalty_inverse(pieces, time_factor):
    rank = time_factor.shape[1]
    half, penalty = kernel_call(
        functools.partial(first_half_kernel, rank // 2),
        [shape((rank, rank)), shape((1, 128))], time_factor, *pieces, flops=6_000_000_000,
    )
    (inverse,) = kernel_call(
        functools.partial(second_half_kernel, rank // 2),
        [shape((rank, rank))], half, flops=6_000_000_000,
    )
    return penalty, inverse


def kernel_call(kernel, out_shape, *args, scratch=(), flops=1_000_000, smem=False):
    spec = pl.BlockSpec(memory_space=pltpu.SMEM) if smem else pl.BlockSpec(memory_space=pltpu.VMEM)
    size = sum(x.size * x.dtype.itemsize for x in (*args, *out_shape))
    return pl.pallas_call(
        kernel,
        out_shape=tuple(out_shape),
        in_specs=[spec] * len(args),
        out_specs=tuple(pl.BlockSpec(memory_space=pltpu.VMEM) for _ in out_shape),
        scratch_shapes=list(scratch),
        compiler_params=ROOM,
        cost_estimate=pl.CostEstimate(flops=flops, bytes_accessed=size, transcendentals=0),
    )(*args)


def shape(dims, dtype=jnp.float32):
    return jax.ShapeDtypeStruct(tuple(dims), dtype)


def swap(x, axis, mask):
    size = lax.axis_size(axis)
    return lax.ppermute(x, axis, [(i, i ^ mask) for i in range(size)])


def swaps(pieces):
    received = list(pieces)
    for d in reversed(range(1, len(pieces))):
        received[d] = swap(pieces[d], "narrow", d)
    return received


def for_each_position(body):
    me = lax.axis_index("narrow")
    for v in range(lax.axis_size("narrow")):
        pl.when(me == v)(functools.partial(body, v))


def rows_of(d, height):
    return pl.ds(pl.multiple_of((lax.axis_index("narrow") ^ d) * height, height), height)


def positions_kernel(coords_ref, user_ref, item_ref, table_ref):
    wide, narrow = lax.axis_index("wide"), lax.axis_index("narrow")
    count = lax.axis_size("narrow")
    for d in range(count):
        tile = wide * count + (narrow ^ d)
        user = user_ref[coords_ref[0, tile]] ^ wide
        item = item_ref[coords_ref[1, tile]] ^ wide
        table_ref[d : d + 1, :] = jnp.full((1, 128), user, jnp.int32)
        table_ref[count + d : count + d + 1, :] = jnp.full((1, 128), item, jnp.int32)


def positions(tile_coords, user_owner, item_owner):
    count = lax.axis_size("narrow")
    (table,) = kernel_call(
        positions_kernel, [shape((2 * count, 128), jnp.int32)],
        tile_coords.T, user_owner, item_owner, smem=True,
    )
    return table[:count], table[count:]


def split_kernel(stack_ref, *outputs):
    width = outputs[0].shape[1]

    def body(v):
        for d, out in enumerate(outputs):
            out[...] = stack_ref[:, (v ^ d) * width : ((v ^ d) + 1) * width]

    for_each_position(body)


def split(stack):
    count = lax.axis_size("narrow")
    height, rows = stack.shape
    return kernel_call(split_kernel, [shape((height, rows // count))] * count, stack)


def store_pair(value, pair_ref):
    rank = value.shape[0]
    rounded = value.astype(pair_ref.dtype)
    pair_ref[:rank] = rounded
    pair_ref[rank:] = (value - rounded.astype(jnp.float32)).astype(pair_ref.dtype)


def pair_kernel(count, *refs):
    pieces, (factor_ref, pair_ref) = refs[:count], refs[count:]
    height = pieces[0].shape[0]
    for d, piece in enumerate(pieces):
        factor_ref[rows_of(d, height), :] = piece[...]
    store_pair(factor_ref[...], pair_ref)


def assemble_kernel(count, *refs):
    factor_ref, pieces, outputs = refs[0], refs[1 : count + 1], refs[count + 1 :]
    height = pieces[0].shape[0] // 3
    for d, piece in enumerate(pieces):
        rows = rows_of(d, height)
        outputs[0][rows, :] = piece[:height] + piece[height : 2 * height]
        outputs[1][rows, :] = piece[height : 2 * height]
        outputs[3][rows, :] = piece[2 * height :]
    outputs[2][...] = factor_ref[...] + outputs[3][...]


def gram_kernel(*refs):
    pairs, (half_ref, rows_ref) = refs[:-2], refs[-2:]
    half, rank = half_ref.shape
    width = pairs[0].shape[1]
    for k, pair in enumerate(pairs):
        rows_ref[:, k * width : (k + 1) * width] = pair[...]
    start = pl.multiple_of(lax.axis_index("wide") % 2 * half, half)
    mine = jnp.concatenate([rows_ref[pl.ds(start + k * rank, half), :] for k in range(2)])
    products = lax.dot_general(
        mine, rows_ref[...], (((1,), (1,)), ((), ())), preferred_element_type=jnp.float32
    )
    rounded = products[:half, :rank]
    mixed = products[:half, rank:] + products[half:, :rank]
    half_ref[...] = rounded + (mixed + products[half:, rank:])


def joint_gram(pairs):
    rank, width = pairs[0].shape[0] // 2, pairs[0].shape[1]
    (total,) = kernel_call(
        gram_kernel, [shape((rank // 2, rank))], *pairs,
        scratch=[pltpu.VMEM((2 * rank, len(pairs) * width), jnp.bfloat16)],
        flops=1_500_000_000,
    )
    mask = 1
    while mask < lax.axis_size("narrow"):
        total = total + swap(total, "narrow", mask)
        mask *= 2
    return total, swap(total, "wide", 1)


def pick_kernel(count, table_ref, *refs):
    pairs, outputs = refs[:-count], refs[-count:]
    for d, out in enumerate(outputs):
        rank = out.shape[0]
        here = table_ref[d : d + 1, :1].astype(jnp.float32).astype(out.dtype)
        here = jnp.broadcast_to(here, out.shape)
        value = pairs[0][:rank]
        for r in range(1, len(pairs)):
            value = jnp.where(here == r, pairs[r][:rank], value)
        out[...] = value


def all_pairs(pair):
    chips = lax.axis_size("wide") // 2
    same = [pair] * chips
    for m in reversed(range(1, chips)):
        same[m] = swap(pair, "wide", 2 * m)
    return [x for a in same for x in (a, swap(a, "wide", 1))]


def fetch_rows(pairs, table):
    count = lax.axis_size("narrow")
    rank, width = pairs[0].shape[0] // 2, pairs[0].shape[1]
    picked = kernel_call(
        functools.partial(pick_kernel, count), [shape((rank, width), jnp.bfloat16)] * count,
        table, *pairs, flops=5_000_000_000,
    )
    return swaps(picked)


def tile_kernel(forward, count, activity_ref, time_ref, *refs):
    pieces, outputs, (stage_ref, sums_ref) = refs[:count], refs[count : 2 * count], refs[2 * count :]
    me = lax.axis_index("narrow")
    for d, piece in enumerate(pieces):
        stage_ref[me ^ d] = piece[...]
    low = jnp.concatenate([stage_ref[q] for q in range(count)], axis=1)
    low = low.astype(jnp.float32)
    times = time_ref[...].T
    total = None
    for k in range(activity_ref.shape[1]):
        khatri = (low * times[:, k : k + 1]).astype(jnp.bfloat16)
        dims = (((1,), (1 if forward else 0,)), ((), ()))
        term = lax.dot_general(khatri, activity_ref[0, k], dims, preferred_element_type=jnp.float32)
        total = term if total is None else total + term
    width = outputs[0].shape[1]
    for q in range(count):
        sums_ref[q] = total[:, q * width : (q + 1) * width]
    for d, out in enumerate(outputs):
        out[...] = sums_ref[me ^ d]


def tile_sums(activity, pieces, time_factor, forward):
    count = len(pieces)
    rank = time_factor.shape[1]
    _, steps, rows, cols = activity.shape
    width = (rows if forward else cols) // count
    return kernel_call(
        functools.partial(tile_kernel, forward, count), [shape((rank, width))] * count,
        activity, time_factor, *pieces,
        scratch=[
            pltpu.VMEM((count, *pieces[0].shape), jnp.bfloat16),
            pltpu.VMEM((count, rank, width), jnp.float32),
        ],
        flops=2 * rank * steps * rows * cols,
    )


def place_kernel(count, table_ref, *refs):
    received, outputs = refs[:count], refs[count:]
    values = [x[...] for x in received]
    for r, out in enumerate(outputs):
        total = None
        for d, value in enumerate(values):
            here = jnp.broadcast_to(table_ref[d : d + 1, :1] == r, value.shape)
            term = jnp.where(here, value, 0.0)
            total = term if total is None else total + term
        out[...] = total


def owner_sums(partials, table):
    received = swaps(partials)
    size = lax.axis_size("wide")
    placed = kernel_call(
        functools.partial(place_kernel, len(received)), [shape(received[0].shape)] * size,
        table, *received,
    )
    order = [*reversed(range(1, size // 2)), 0]
    arrived = {m: swap(placed[2 * m + 1], "wide", 1) for m in order}
    terms = [placed[0], arrived[0]]
    for m in order[:-1]:
        terms.append(swap(placed[2 * m] + arrived[m], "wide", 2 * m))
    return terms


def update_kernel(terms, count, *refs):
    sums = refs[0][...]
    for term in refs[1:terms]:
        sums = sums + term[...]
    shifted_ref, dual_ref, penalty_ref, inverse_ref = refs[terms : terms + 4]
    outputs = refs[terms + 4 :]
    value_ref = outputs[-1]
    penalty = penalty_ref[:1, :1]
    inverse = inverse_ref[...]
    shifted, dual = shifted_ref[...], dual_ref[...]
    for _ in range(PASSES):
        target = jnp.dot(
            inverse, sums + penalty * shifted, precision=HIGHEST, preferred_element_type=jnp.float32
        )
        value = target - dual
        dual = jnp.maximum(-value, 0.0)
        shifted = jnp.abs(value)
    value_ref[...] = value
    height = outputs[0].shape[0]
    for d in range(count):
        outputs[d][...] = value_ref[rows_of(d, height), :]
    if len(outputs) > count + 1:
        store_pair(jnp.maximum(value, 0.0), outputs[count])


def admm(terms, shifted, dual, penalty, inverse, more):
    count = lax.axis_size("narrow")
    rank, width = shifted.shape
    out = [shape((rank // count, width))] * count
    if more:
        out += [shape((2 * rank, width), jnp.bfloat16)]
    return kernel_call(
        functools.partial(update_kernel, len(terms), count), out,
        *terms, shifted, dual, penalty, inverse,
        scratch=[pltpu.VMEM((rank, width), jnp.float32)],
        flops=12 * rank * rank * width * PASSES,
    )


def final_kernel(count, *refs):
    pieces, (factor_ref, dual_ref) = refs[:count], refs[count:]
    width = pieces[0].shape[1]

    def body(v):
        for d, piece in enumerate(pieces):
            lanes = slice((v ^ d) * width, ((v ^ d) + 1) * width)
            value = piece[...]
            factor_ref[:, lanes] = jnp.maximum(value, 0.0)
            dual_ref[:, lanes] = jnp.maximum(-value, 0.0)

    for_each_position(body)


def to_columns(pieces):
    received = swaps(pieces)
    height, width = received[0].shape
    count = len(received)
    factor, dual = kernel_call(
        functools.partial(final_kernel, count), [shape((height, count * width))] * 2,
        *received,
    )
    return factor.T, dual.T


def local(
    activity,
    tile_coords,
    user_owner,
    item_owner,
    user_factor,
    item_factor,
    time_factor,
    user_dual,
    item_dual,
):
    return sweep(
        activity, tile_coords, user_owner, item_owner, user_factor.T, item_factor.T,
        time_factor, user_dual.T, item_dual.T,
    )


def sweep(
    activity, tile_coords, user_owner, item_owner, user_factor, item_factor, time_factor,
    user_dual, item_dual,
):
    rank = time_factor.shape[1]
    count = lax.axis_size("narrow")
    user_table, item_table = positions(tile_coords, user_owner, item_owner)

    pieces = swaps(split(item_factor))
    rows = shape((rank, pieces[0].shape[1]))
    pair = shape((2 * rank, rows.shape[1]), jnp.bfloat16)
    item_rows, pair = kernel_call(functools.partial(pair_kernel, count), [rows, pair], *pieces)
    stack = jnp.concatenate([user_factor, user_dual, item_dual])
    user_shifted, udual_rows, item_shifted, idual_rows = kernel_call(
        functools.partial(assemble_kernel, count), [rows] * 4,
        item_rows, *swaps(split(stack)),
    )

    pairs = all_pairs(pair)
    partials = tile_sums(activity, fetch_rows(pairs, item_table), time_factor, True)
    terms = owner_sums(partials, user_table)
    penalty, inverse = penalty_inverse(joint_gram(pairs), time_factor)
    *user_pieces, pair = admm(terms, user_shifted, udual_rows, penalty, inverse, True)

    pairs = all_pairs(pair)
    partials = tile_sums(activity, fetch_rows(pairs, user_table), time_factor, False)
    terms = owner_sums(partials, item_table)
    penalty, inverse = penalty_inverse(joint_gram(pairs), time_factor)
    new_users, new_user_dual = to_columns(user_pieces)
    item_pieces = admm(terms, item_shifted, idual_rows, penalty, inverse, False)
    new_items, new_item_dual = to_columns(item_pieces)
    return (new_users, new_items, new_user_dual, new_item_dual)


def solution(mesh):
    in_specs = (
        P(("wide", "narrow"), None, None, None),
        P(),
        P(),
        P(),
        P("wide", "narrow"),
        P("wide", "narrow"),
        P(),
        P("wide", "narrow"),
        P("wide", "narrow"),
    )
    out_specs = (P("wide", "narrow"), P("wide", "narrow"), P("wide", "narrow"), P("wide", "narrow"))
    return jax.shard_map(local, mesh=mesh, in_specs=in_specs, out_specs=out_specs, check_vma=False)
```

```python
import functools

import jax
import jax.numpy as jnp
from jax import lax
from jax.experimental import pallas as pl
from jax.experimental.pallas import tpu as pltpu
from jax.sharding import PartitionSpec as P


PASSES = 2
LEAF = 8
HIGHEST = lax.Precision.HIGHEST
ROOM = pltpu.CompilerParams(vmem_limit_bytes=16 * 2**20)


def eliminate(left, right):
    panel, width = left.shape
    lane = lax.broadcasted_iota(jnp.int32, (LEAF, width), 1)
    sub = lax.broadcasted_iota(jnp.int32, (LEAF, width), 0)
    for j in range(0, panel, LEAF):
        cols = [jnp.broadcast_to(left[:, j + m : j + m + 1], (panel, width)) for m in range(LEAF)]
        d = [c[j : j + LEAF] for c in cols]
        for k in range(LEAF):
            r = 1.0 / d[k][k : k + 1]
            pivot = d[k]
            here = sub == k
            for m in range(LEAF):
                if m != k:
                    f = d[m][k : k + 1] * r
                    d[m] = jnp.where(here, f, d[m] - pivot * f)
            d[k] = jnp.where(here, r, -pivot * r)
        inside = (lane >= j) & (lane < j + LEAF)
        el = jnp.where(inside, jnp.where(lane == sub + j, 1.0, 0.0), left[j : j + LEAF])
        er = right[j : j + LEAF]
        rl = sum(d[m] * el[m : m + 1] for m in range(LEAF))
        rr = sum(d[m] * er[m : m + 1] for m in range(LEAF))
        new_left, new_right = [], []
        for i in range(0, panel, LEAF):
            if i == j:
                new_left.append(rl)
                new_right.append(rr)
            else:
                c = [col[i : i + LEAF] for col in cols]
                ul = sum(c[m] * rl[m : m + 1] for m in range(LEAF))
                ur = sum(c[m] * rr[m : m + 1] for m in range(LEAF))
                new_left.append(jnp.where(inside, 0.0, left[i : i + LEAF]) - ul)
                new_right.append(right[i : i + LEAF] - ur)
        left = jnp.concatenate(new_left, 0)
        right = jnp.concatenate(new_right, 0)
    return left, right


def eliminate_panel(panel, k, work_ref):
    rank = work_ref.shape[0]
    half = rank // 2
    lane = lax.broadcasted_iota(jnp.int32, (1, rank), 1)
    rows = pl.ds(k * panel, panel)
    left, right = eliminate(work_ref[rows, :half], work_ref[rows, half:])
    done = jnp.concatenate([left, right], 1)
    full = work_ref[...]
    change = jnp.dot(full[:, :panel], done, precision=HIGHEST, preferred_element_type=jnp.float32)
    work_ref[...] = pltpu.roll(jnp.where(lane < panel, 0.0, full) - change, rank - panel, 1)
    work_ref[rows, :] = pltpu.roll(done, rank - panel, 1)


def first_half_kernel(panel, time_ref, *refs):
    pieces, (work_ref, penalty_ref) = refs[:-2], refs[-2:]
    rank = work_ref.shape[0]
    half = rank // 2
    mine, other = (piece[...] for piece in pieces)
    first = jnp.broadcast_to(lax.axis_index("wide") % 2 == 0, mine.shape)
    quadrants = unpack(jnp.where(first, mine, other), jnp.where(first, other, mine))
    for k, quadrant in enumerate(quadrants):
        row, col = k // 2 * half, k % 2 * half
        work_ref[row : row + half, col : col + half] = quadrant
    time = time_ref[...]
    times = lax.dot_general(
        time, time, (((0,), (0,)), ((), ())), precision=HIGHEST, preferred_element_type=jnp.float32
    )
    gram = work_ref[...] * times
    row = lax.broadcasted_iota(jnp.int32, (rank, rank), 0)
    col = lax.broadcasted_iota(jnp.int32, (rank, rank), 1)
    trace = jnp.sum(jnp.where(row == col, gram, 0.0), axis=0, keepdims=True)
    penalty = jnp.sum(trace, axis=1, keepdims=True) / rank
    penalty_ref[...] = jnp.broadcast_to(penalty, penalty_ref.shape)
    work_ref[...] = gram + jnp.where(row == col, penalty, 0.0)
    eliminate_panel(panel, 0, work_ref)


def second_half_kernel(panel, half_ref, inverse_ref):
    inverse_ref[...] = half_ref[...]
    eliminate_panel(panel, 1, inverse_ref)


def penalty_inverse(pieces, time_factor):
    rank = time_factor.shape[1]
    half, penalty = kernel_call(
        functools.partial(first_half_kernel, rank // 2),
        [shape((rank, rank)), shape((1, 128))], time_factor, *pieces, flops=6_000_000_000,
    )
    (inverse,) = kernel_call(
        functools.partial(second_half_kernel, rank // 2),
        [shape((rank, rank))], half, flops=6_000_000_000,
    )
    return penalty, inverse


def kernel_call(kernel, out_shape, *args, scratch=(), flops=1_000_000, smem=False):
    spec = pl.BlockSpec(memory_space=pltpu.SMEM) if smem else pl.BlockSpec(memory_space=pltpu.VMEM)
    size = sum(x.size * x.dtype.itemsize for x in (*args, *out_shape))
    return pl.pallas_call(
        kernel,
        out_shape=tuple(out_shape),
        in_specs=[spec] * len(args),
        out_specs=tuple(pl.BlockSpec(memory_space=pltpu.VMEM) for _ in out_shape),
        scratch_shapes=list(scratch),
        compiler_params=ROOM,
        cost_estimate=pl.CostEstimate(flops=flops, bytes_accessed=size, transcendentals=0),
    )(*args)


def shape(dims, dtype=jnp.float32):
    return jax.ShapeDtypeStruct(tuple(dims), dtype)


def swap(x, axis, mask):
    size = lax.axis_size(axis)
    return lax.ppermute(x, axis, [(i, i ^ mask) for i in range(size)])


def swaps(pieces):
    received = list(pieces)
    for d in reversed(range(1, len(pieces))):
        received[d] = swap(pieces[d], "narrow", d)
    return received


def for_each_position(body):
    me = lax.axis_index("narrow")
    for v in range(lax.axis_size("narrow")):
        pl.when(me == v)(functools.partial(body, v))


def rows_of(d, height):
    return pl.ds(pl.multiple_of((lax.axis_index("narrow") ^ d) * height, height), height)


def positions_kernel(coords_ref, user_ref, item_ref, table_ref):
    wide, narrow = lax.axis_index("wide"), lax.axis_index("narrow")
    count = lax.axis_size("narrow")
    for d in range(count):
        tile = wide * count + (narrow ^ d)
        user = user_ref[coords_ref[0, tile]] ^ wide
        item = item_ref[coords_ref[1, tile]] ^ wide
        table_ref[d : d + 1, :] = jnp.full((1, 128), user, jnp.int32)
        table_ref[count + d : count + d + 1, :] = jnp.full((1, 128), item, jnp.int32)


def positions(tile_coords, user_owner, item_owner):
    count = lax.axis_size("narrow")
    (table,) = kernel_call(
        positions_kernel, [shape((2 * count, 128), jnp.int32)],
        tile_coords.T, user_owner, item_owner, smem=True,
    )
    return table[:count], table[count:]


def split_kernel(stack_ref, *outputs):
    width = outputs[0].shape[1]

    def body(v):
        for d, out in enumerate(outputs):
            out[...] = stack_ref[:, (v ^ d) * width : ((v ^ d) + 1) * width]

    for_each_position(body)


def split(stack):
    count = lax.axis_size("narrow")
    height, rows = stack.shape
    return kernel_call(split_kernel, [shape((height, rows // count))] * count, stack)


def store_pair(value, pair_ref):
    rank = value.shape[0]
    rounded = value.astype(pair_ref.dtype)
    pair_ref[:rank] = rounded
    pair_ref[rank:] = (value - rounded.astype(jnp.float32)).astype(pair_ref.dtype)


def pair_kernel(count, *refs):
    pieces, (factor_ref, pair_ref) = refs[:count], refs[count:]
    height = pieces[0].shape[0]
    for d, piece in enumerate(pieces):
        factor_ref[rows_of(d, height), :] = piece[...]
    store_pair(factor_ref[...], pair_ref)


def assemble_kernel(count, *refs):
    factor_ref, pieces, outputs = refs[0], refs[1 : count + 1], refs[count + 1 :]
    height = pieces[0].shape[0] // 3
    for d, piece in enumerate(pieces):
        rows = rows_of(d, height)
        outputs[0][rows, :] = piece[:height] + piece[height : 2 * height]
        outputs[1][rows, :] = piece[height : 2 * height]
        outputs[3][rows, :] = piece[2 * height :]
    outputs[2][...] = factor_ref[...] + outputs[3][...]


def pack(core, rows):
    half = rows.shape[0]
    part = half // 2
    left = lax.broadcasted_iota(jnp.int32, (1, half), 1) < part
    own = rows[:, core * half : (core + 1) * half]
    other = rows[:, (1 - core) * half : (2 - core) * half]
    first, second = (other[:part], other[part:]) if core == 0 else (other[part:], other[:part])
    turned = pltpu.roll(second[part // 2 :], part, 1)
    return jnp.concatenate(
        [
            own[:part],
            jnp.where(left, first, own[part:]),
            jnp.where(left, turned, second[: part // 2]),
        ]
    )


def unpack(a, b):
    half = a.shape[1]
    part = half // 2
    left = lax.broadcasted_iota(jnp.int32, (1, half), 1) < part

    def last(x):
        return jnp.concatenate([x[half:], pltpu.roll(x[half:], part, 1)])

    a_turned, b_turned = a[:half].T, b[:half].T
    b_last = last(b)
    b_last_turned = jnp.concatenate([b_last, b_last]).T
    upper_left = jnp.concatenate([a[:part], a_turned[part:]])
    lower_right = jnp.concatenate([b[:part], b_turned[part:]])
    upper_right = jnp.concatenate(
        [
            jnp.where(left, a[part:half], b_turned[:part]),
            jnp.where(left, b_last_turned[part:], last(a)),
        ]
    )
    return upper_left, upper_right, upper_right.T, lower_right


def gram_kernel(*refs):
    pairs, (packed_ref, rows_ref) = refs[:-2], refs[-2:]
    rank = rows_ref.shape[0] // 2
    half = rank // 2
    width = pairs[0].shape[1]
    for k, pair in enumerate(pairs):
        rows_ref[:, k * width : (k + 1) * width] = pair[...]
    start = pl.multiple_of(lax.axis_index("wide") % 2 * half, half)
    mine = jnp.concatenate([rows_ref[pl.ds(start + k * rank, half), :] for k in range(2)])
    products = lax.dot_general(
        mine, rows_ref[...], (((1,), (1,)), ((), ())), preferred_element_type=jnp.float32
    )
    rounded = products[:half, :rank]
    mixed = products[:half, rank:] + products[half:, :rank]
    gram = rounded + (mixed + products[half:, rank:])
    for core in range(2):

        @pl.when(lax.axis_index("wide") % 2 == core)
        def _(core=core):
            packed_ref[...] = pack(core, gram)


def joint_gram(pairs):
    rank, width = pairs[0].shape[0] // 2, pairs[0].shape[1]
    (total,) = kernel_call(
        gram_kernel, [shape((rank // 2 + rank // 8, rank // 2))], *pairs,
        scratch=[pltpu.VMEM((2 * rank, len(pairs) * width), jnp.bfloat16)],
        flops=1_500_000_000,
    )
    mask = 1
    while mask < lax.axis_size("narrow"):
        total = total + swap(total, "narrow", mask)
        mask *= 2
    return total, swap(total, "wide", 1)


def pick_kernel(count, table_ref, *refs):
    pairs, outputs = refs[:-count], refs[-count:]
    for d, out in enumerate(outputs):
        rank = out.shape[0]
        here = table_ref[d : d + 1, :1].astype(jnp.float32).astype(out.dtype)
        here = jnp.broadcast_to(here, out.shape)
        value = pairs[0][:rank]
        for r in range(1, len(pairs)):
            value = jnp.where(here == r, pairs[r][:rank], value)
        out[...] = value


def all_pairs(pair):
    chips = lax.axis_size("wide") // 2
    same = [pair] * chips
    for m in reversed(range(1, chips)):
        same[m] = swap(pair, "wide", 2 * m)
    return [x for a in same for x in (a, swap(a, "wide", 1))]


def fetch_rows(pairs, table):
    count = lax.axis_size("narrow")
    rank, width = pairs[0].shape[0] // 2, pairs[0].shape[1]
    picked = kernel_call(
        functools.partial(pick_kernel, count), [shape((rank, width), jnp.bfloat16)] * count,
        table, *pairs, flops=5_000_000_000,
    )
    return swaps(picked)


def tile_kernel(forward, count, activity_ref, time_ref, *refs):
    pieces, outputs, (stage_ref, sums_ref) = refs[:count], refs[count : 2 * count], refs[2 * count :]
    me = lax.axis_index("narrow")
    for d, piece in enumerate(pieces):
        stage_ref[me ^ d] = piece[...]
    low = jnp.concatenate([stage_ref[q] for q in range(count)], axis=1)
    low = low.astype(jnp.float32)
    times = time_ref[...].T
    total = None
    for k in range(activity_ref.shape[1]):
        khatri = (low * times[:, k : k + 1]).astype(jnp.bfloat16)
        dims = (((1,), (1 if forward else 0,)), ((), ()))
        term = lax.dot_general(khatri, activity_ref[0, k], dims, preferred_element_type=jnp.float32)
        total = term if total is None else total + term
    width = outputs[0].shape[1]
    for q in range(count):
        sums_ref[q] = total[:, q * width : (q + 1) * width]
    for d, out in enumerate(outputs):
        out[...] = sums_ref[me ^ d]


def tile_sums(activity, pieces, time_factor, forward):
    count = len(pieces)
    rank = time_factor.shape[1]
    _, steps, rows, cols = activity.shape
    width = (rows if forward else cols) // count
    return kernel_call(
        functools.partial(tile_kernel, forward, count), [shape((rank, width))] * count,
        activity, time_factor, *pieces,
        scratch=[
            pltpu.VMEM((count, *pieces[0].shape), jnp.bfloat16),
            pltpu.VMEM((count, rank, width), jnp.float32),
        ],
        flops=2 * rank * steps * rows * cols,
    )


def place_kernel(count, table_ref, *refs):
    received, outputs = refs[:count], refs[count:]
    values = [x[...] for x in received]
    for r, out in enumerate(outputs):
        total = None
        for d, value in enumerate(values):
            here = jnp.broadcast_to(table_ref[d : d + 1, :1] == r, value.shape)
            term = jnp.where(here, value, 0.0)
            total = term if total is None else total + term
        out[...] = total


def owner_sums(partials, table):
    received = swaps(partials)
    size = lax.axis_size("wide")
    placed = kernel_call(
        functools.partial(place_kernel, len(received)), [shape(received[0].shape)] * size,
        table, *received,
    )
    order = [*reversed(range(1, size // 2)), 0]
    arrived = {m: swap(placed[2 * m + 1], "wide", 1) for m in order}
    terms = [placed[0], arrived[0]]
    for m in order[:-1]:
        terms.append(swap(placed[2 * m] + arrived[m], "wide", 2 * m))
    return terms


def update_kernel(terms, count, *refs):
    sums = refs[0][...]
    for term in refs[1:terms]:
        sums = sums + term[...]
    shifted_ref, dual_ref, penalty_ref, inverse_ref = refs[terms : terms + 4]
    outputs = refs[terms + 4 :]
    value_ref = outputs[-1]
    penalty = penalty_ref[:1, :1]
    inverse = inverse_ref[...]
    shifted, dual = shifted_ref[...], dual_ref[...]
    for _ in range(PASSES):
        target = jnp.dot(
            inverse, sums + penalty * shifted, precision=HIGHEST, preferred_element_type=jnp.float32
        )
        value = target - dual
        dual = jnp.maximum(-value, 0.0)
        shifted = jnp.abs(value)
    value_ref[...] = value
    height = outputs[0].shape[0]
    for d in range(count):
        outputs[d][...] = value_ref[rows_of(d, height), :]
    if len(outputs) > count + 1:
        store_pair(jnp.maximum(value, 0.0), outputs[count])


def admm(terms, shifted, dual, penalty, inverse, more):
    count = lax.axis_size("narrow")
    rank, width = shifted.shape
    out = [shape((rank // count, width))] * count
    if more:
        out += [shape((2 * rank, width), jnp.bfloat16)]
    return kernel_call(
        functools.partial(update_kernel, len(terms), count), out,
        *terms, shifted, dual, penalty, inverse,
        scratch=[pltpu.VMEM((rank, width), jnp.float32)],
        flops=12 * rank * rank * width * PASSES,
    )


def final_kernel(count, *refs):
    pieces, (factor_ref, dual_ref) = refs[:count], refs[count:]
    width = pieces[0].shape[1]

    def body(v):
        for d, piece in enumerate(pieces):
            lanes = slice((v ^ d) * width, ((v ^ d) + 1) * width)
            value = piece[...]
            factor_ref[:, lanes] = jnp.maximum(value, 0.0)
            dual_ref[:, lanes] = jnp.maximum(-value, 0.0)

    for_each_position(body)


def to_columns(pieces):
    received = swaps(pieces)
    height, width = received[0].shape
    count = len(received)
    factor, dual = kernel_call(
        functools.partial(final_kernel, count), [shape((height, count * width))] * 2,
        *received,
    )
    return factor.T, dual.T


def local(
    activity,
    tile_coords,
    user_owner,
    item_owner,
    user_factor,
    item_factor,
    time_factor,
    user_dual,
    item_dual,
):
    return sweep(
        activity, tile_coords, user_owner, item_owner, user_factor.T, item_factor.T,
        time_factor, user_dual.T, item_dual.T,
    )


def sweep(
    activity, tile_coords, user_owner, item_owner, user_factor, item_factor, time_factor,
    user_dual, item_dual,
):
    rank = time_factor.shape[1]
    count = lax.axis_size("narrow")
    user_table, item_table = positions(tile_coords, user_owner, item_owner)

    pieces = swaps(split(item_factor))
    rows = shape((rank, pieces[0].shape[1]))
    pair = shape((2 * rank, rows.shape[1]), jnp.bfloat16)
    item_rows, pair = kernel_call(functools.partial(pair_kernel, count), [rows, pair], *pieces)
    stack = jnp.concatenate([user_factor, user_dual, item_dual])
    user_shifted, udual_rows, item_shifted, idual_rows = kernel_call(
        functools.partial(assemble_kernel, count), [rows] * 4,
        item_rows, *swaps(split(stack)),
    )

    pairs = all_pairs(pair)
    partials = tile_sums(activity, fetch_rows(pairs, item_table), time_factor, True)
    terms = owner_sums(partials, user_table)
    penalty, inverse = penalty_inverse(joint_gram(pairs), time_factor)
    *user_pieces, pair = admm(terms, user_shifted, udual_rows, penalty, inverse, True)

    pairs = all_pairs(pair)
    partials = tile_sums(activity, fetch_rows(pairs, user_table), time_factor, False)
    terms = owner_sums(partials, item_table)
    penalty, inverse = penalty_inverse(joint_gram(pairs), time_factor)
    new_users, new_user_dual = to_columns(user_pieces)
    item_pieces = admm(terms, item_shifted, idual_rows, penalty, inverse, False)
    new_items, new_item_dual = to_columns(item_pieces)
    return (new_users, new_items, new_user_dual, new_item_dual)


def solution(mesh):
    in_specs = (
        P(("wide", "narrow"), None, None, None),
        P(),
        P(),
        P(),
        P("wide", "narrow"),
        P("wide", "narrow"),
        P(),
        P("wide", "narrow"),
        P("wide", "narrow"),
    )
    out_specs = (P("wide", "narrow"), P("wide", "narrow"), P("wide", "narrow"), P("wide", "narrow"))
    return jax.shard_map(local, mesh=mesh, in_specs=in_specs, out_specs=out_specs, check_vma=False)
```

```python
import functools

import jax
import jax.numpy as jnp
from jax import lax
from jax.experimental import pallas as pl
from jax.experimental.pallas import tpu as pltpu
from jax.sharding import PartitionSpec as P


PASSES = 2
LEAF = 8
HIGHEST = lax.Precision.HIGHEST
ROOM = pltpu.CompilerParams(vmem_limit_bytes=16 * 2**20)


def eliminate(left, right):
    panel, width = left.shape
    lane = lax.broadcasted_iota(jnp.int32, (LEAF, width), 1)
    sub = lax.broadcasted_iota(jnp.int32, (LEAF, width), 0)
    for j in range(0, panel, LEAF):
        cols = [jnp.broadcast_to(left[:, j + m : j + m + 1], (panel, width)) for m in range(LEAF)]
        d = [c[j : j + LEAF] for c in cols]
        for k in range(LEAF):
            r = 1.0 / d[k][k : k + 1]
            pivot = d[k]
            here = sub == k
            for m in range(LEAF):
                if m != k:
                    f = d[m][k : k + 1] * r
                    d[m] = jnp.where(here, f, d[m] - pivot * f)
            d[k] = jnp.where(here, r, -pivot * r)
        inside = (lane >= j) & (lane < j + LEAF)
        el = jnp.where(inside, jnp.where(lane == sub + j, 1.0, 0.0), left[j : j + LEAF])
        er = right[j : j + LEAF]
        rl = sum(d[m] * el[m : m + 1] for m in range(LEAF))
        rr = sum(d[m] * er[m : m + 1] for m in range(LEAF))
        new_left, new_right = [], []
        for i in range(0, panel, LEAF):
            if i == j:
                new_left.append(rl)
                new_right.append(rr)
            else:
                c = [col[i : i + LEAF] for col in cols]
                ul = sum(c[m] * rl[m : m + 1] for m in range(LEAF))
                ur = sum(c[m] * rr[m : m + 1] for m in range(LEAF))
                new_left.append(jnp.where(inside, 0.0, left[i : i + LEAF]) - ul)
                new_right.append(right[i : i + LEAF] - ur)
        left = jnp.concatenate(new_left, 0)
        right = jnp.concatenate(new_right, 0)
    return left, right


def eliminate_panel(panel, k, work_ref):
    rank = work_ref.shape[0]
    half = rank // 2
    lane = lax.broadcasted_iota(jnp.int32, (1, rank), 1)
    rows = pl.ds(k * panel, panel)
    left, right = eliminate(work_ref[rows, :half], work_ref[rows, half:])
    done = jnp.concatenate([left, right], 1)
    full = work_ref[...]
    change = jnp.dot(full[:, :panel], done, precision=HIGHEST, preferred_element_type=jnp.float32)
    work_ref[...] = pltpu.roll(jnp.where(lane < panel, 0.0, full) - change, rank - panel, 1)
    work_ref[rows, :] = pltpu.roll(done, rank - panel, 1)


def first_half_kernel(panel, time_ref, *refs):
    pieces, (work_ref, penalty_ref) = refs[:-2], refs[-2:]
    rank = work_ref.shape[0]
    half = rank // 2
    mine, other = (piece[...] for piece in pieces)
    first = jnp.broadcast_to(lax.axis_index("wide") % 2 == 0, mine.shape)
    quadrants = unpack(jnp.where(first, mine, other), jnp.where(first, other, mine))
    for k, quadrant in enumerate(quadrants):
        row, col = k // 2 * half, k % 2 * half
        work_ref[row : row + half, col : col + half] = quadrant
    time = time_ref[...]
    times = lax.dot_general(
        time, time, (((0,), (0,)), ((), ())), precision=HIGHEST, preferred_element_type=jnp.float32
    )
    gram = work_ref[...] * times
    row = lax.broadcasted_iota(jnp.int32, (rank, rank), 0)
    col = lax.broadcasted_iota(jnp.int32, (rank, rank), 1)
    trace = jnp.sum(jnp.where(row == col, gram, 0.0), axis=0, keepdims=True)
    penalty = jnp.sum(trace, axis=1, keepdims=True) / rank
    penalty_ref[...] = jnp.broadcast_to(penalty, penalty_ref.shape)
    work_ref[...] = gram + jnp.where(row == col, penalty, 0.0)
    eliminate_panel(panel, 0, work_ref)


def second_half_kernel(panel, half_ref, inverse_ref):
    inverse_ref[...] = half_ref[...]
    eliminate_panel(panel, 1, inverse_ref)


def penalty_inverse(pieces, time_factor):
    rank = time_factor.shape[1]
    half, penalty = kernel_call(
        functools.partial(first_half_kernel, rank // 2),
        [shape((rank, rank)), shape((1, 128))], time_factor, *pieces, flops=6_000_000_000,
    )
    (inverse,) = kernel_call(
        functools.partial(second_half_kernel, rank // 2),
        [shape((rank, rank))], half, flops=6_000_000_000,
    )
    return penalty, inverse


def kernel_call(kernel, out_shape, *args, scratch=(), flops=1_000_000, smem=False):
    spec = pl.BlockSpec(memory_space=pltpu.SMEM) if smem else pl.BlockSpec(memory_space=pltpu.VMEM)
    size = sum(x.size * x.dtype.itemsize for x in (*args, *out_shape))
    return pl.pallas_call(
        kernel,
        out_shape=tuple(out_shape),
        in_specs=[spec] * len(args),
        out_specs=tuple(pl.BlockSpec(memory_space=pltpu.VMEM) for _ in out_shape),
        scratch_shapes=list(scratch),
        compiler_params=ROOM,
        cost_estimate=pl.CostEstimate(flops=flops, bytes_accessed=size, transcendentals=0),
    )(*args)


def shape(dims, dtype=jnp.float32):
    return jax.ShapeDtypeStruct(tuple(dims), dtype)


def swap(x, axis, mask):
    size = lax.axis_size(axis)
    return lax.ppermute(x, axis, [(i, i ^ mask) for i in range(size)])


def swaps(pieces):
    received = list(pieces)
    for d in reversed(range(1, len(pieces))):
        received[d] = swap(pieces[d], "narrow", d)
    return received


def for_each_position(body):
    me = lax.axis_index("narrow")
    for v in range(lax.axis_size("narrow")):
        pl.when(me == v)(functools.partial(body, v))


def rows_of(d, height):
    return pl.ds(pl.multiple_of((lax.axis_index("narrow") ^ d) * height, height), height)


def positions_kernel(coords_ref, user_ref, item_ref, table_ref):
    wide, narrow = lax.axis_index("wide"), lax.axis_index("narrow")
    count = lax.axis_size("narrow")
    for d in range(count):
        tile = wide * count + (narrow ^ d)
        user = user_ref[coords_ref[0, tile]] ^ wide
        item = item_ref[coords_ref[1, tile]] ^ wide
        table_ref[d : d + 1, :] = jnp.full((1, 128), user, jnp.int32)
        table_ref[count + d : count + d + 1, :] = jnp.full((1, 128), item, jnp.int32)


def positions(tile_coords, user_owner, item_owner):
    count = lax.axis_size("narrow")
    (table,) = kernel_call(
        positions_kernel, [shape((2 * count, 128), jnp.int32)],
        tile_coords.T, user_owner, item_owner, smem=True,
    )
    return table[:count], table[count:]


def split_kernel(stack_ref, *outputs):
    width = outputs[0].shape[1]

    def body(v):
        for d, out in enumerate(outputs):
            out[...] = stack_ref[:, (v ^ d) * width : ((v ^ d) + 1) * width]

    for_each_position(body)


def split(stack):
    count = lax.axis_size("narrow")
    height, rows = stack.shape
    return kernel_call(split_kernel, [shape((height, rows // count))] * count, stack)


def store_pair(value, pair_ref):
    rank = value.shape[0]
    rounded = value.astype(pair_ref.dtype)
    pair_ref[:rank] = rounded
    pair_ref[rank:] = (value - rounded.astype(jnp.float32)).astype(pair_ref.dtype)


def pair_kernel(count, *refs):
    pieces, (factor_ref, pair_ref) = refs[:count], refs[count:]
    height = pieces[0].shape[0]
    for d, piece in enumerate(pieces):
        factor_ref[rows_of(d, height), :] = piece[...]
    store_pair(factor_ref[...], pair_ref)


def assemble_kernel(count, *refs):
    factor_ref, pieces, outputs = refs[0], refs[1 : count + 1], refs[count + 1 :]
    height = pieces[0].shape[0] // 3
    for d, piece in enumerate(pieces):
        rows = rows_of(d, height)
        outputs[0][rows, :] = piece[:height] + piece[height : 2 * height]
        outputs[1][rows, :] = piece[height : 2 * height]
        outputs[3][rows, :] = piece[2 * height :]
    outputs[2][...] = factor_ref[...] + outputs[3][...]


def pack(core, rows):
    half = rows.shape[0]
    part = half // 2
    left = lax.broadcasted_iota(jnp.int32, (1, half), 1) < part
    own = rows[:, core * half : (core + 1) * half]
    other = rows[:, (1 - core) * half : (2 - core) * half]
    first, second = (other[:part], other[part:]) if core == 0 else (other[part:], other[:part])
    turned = pltpu.roll(second[part // 2 :], part, 1)
    return jnp.concatenate(
        [
            own[:part],
            jnp.where(left, first, own[part:]),
            jnp.where(left, turned, second[: part // 2]),
        ]
    )


def unpack(a, b):
    half = a.shape[1]
    part = half // 2
    left = lax.broadcasted_iota(jnp.int32, (1, half), 1) < part

    def last(x):
        return jnp.concatenate([x[half:], pltpu.roll(x[half:], part, 1)])

    a_turned, b_turned = a[:half].T, b[:half].T
    b_last = last(b)
    b_last_turned = jnp.concatenate([b_last, b_last]).T
    upper_left = jnp.concatenate([a[:part], a_turned[part:]])
    lower_right = jnp.concatenate([b[:part], b_turned[part:]])
    upper_right = jnp.concatenate(
        [
            jnp.where(left, a[part:half], b_turned[:part]),
            jnp.where(left, b_last_turned[part:], last(a)),
        ]
    )
    return upper_left, upper_right, upper_right.T, lower_right


def gram_kernel(*refs):
    pairs, (packed_ref, rows_ref) = refs[:-2], refs[-2:]
    rank = rows_ref.shape[0] // 2
    half = rank // 2
    width = pairs[0].shape[1]
    for k, pair in enumerate(pairs):
        rows_ref[:, k * width : (k + 1) * width] = pair[...]
    start = pl.multiple_of(lax.axis_index("wide") % 2 * half, half)
    mine = jnp.concatenate([rows_ref[pl.ds(start + k * rank, half), :] for k in range(2)])
    products = lax.dot_general(
        mine, rows_ref[...], (((1,), (1,)), ((), ())), preferred_element_type=jnp.float32
    )
    rounded = products[:half, :rank]
    mixed = products[:half, rank:] + products[half:, :rank]
    gram = rounded + (mixed + products[half:, rank:])
    for core in range(2):

        @pl.when(lax.axis_index("wide") % 2 == core)
        def _(core=core):
            packed_ref[...] = pack(core, gram)


def joint_gram(pairs):
    rank, width = pairs[0].shape[0] // 2, pairs[0].shape[1]
    (total,) = kernel_call(
        gram_kernel, [shape((rank // 2 + rank // 8, rank // 2))], *pairs,
        scratch=[pltpu.VMEM((2 * rank, len(pairs) * width), jnp.bfloat16)],
        flops=1_500_000_000,
    )
    mask = 1
    while mask < lax.axis_size("narrow"):
        total = total + swap(total, "narrow", mask)
        mask *= 2
    return total, swap(total, "wide", 1)


def pick_kernel(count, table_ref, *refs):
    pairs, outputs = refs[:-count], refs[-count:]
    for d, out in enumerate(outputs):
        rank = out.shape[0]
        here = table_ref[d : d + 1, :1].astype(jnp.float32).astype(out.dtype)
        here = jnp.broadcast_to(here, out.shape)
        value = pairs[0][:rank]
        for r in range(1, len(pairs)):
            value = jnp.where(here == r, pairs[r][:rank], value)
        out[...] = value


def all_pairs(pair):
    chips = lax.axis_size("wide") // 2
    same = [pair] * chips
    for m in reversed(range(1, chips)):
        same[m] = swap(pair, "wide", 2 * m)
    return [x for a in same for x in (a, swap(a, "wide", 1))]


def fetch_rows(pairs, table):
    count = lax.axis_size("narrow")
    rank, width = pairs[0].shape[0] // 2, pairs[0].shape[1]
    picked = kernel_call(
        functools.partial(pick_kernel, count), [shape((rank, width), jnp.bfloat16)] * count,
        table, *pairs, flops=5_000_000_000,
    )
    return swaps(picked)


def tile_kernel(forward, count, activity_ref, time_ref, *refs):
    pieces, outputs, (stage_ref, sums_ref) = refs[:count], refs[count : 2 * count], refs[2 * count :]
    me = lax.axis_index("narrow")
    for d, piece in enumerate(pieces):
        stage_ref[me ^ d] = piece[...]
    low = jnp.concatenate([stage_ref[q] for q in range(count)], axis=1)
    low = low.astype(jnp.float32)
    times = time_ref[...].T
    total = None
    for k in range(activity_ref.shape[1]):
        khatri = (low * times[:, k : k + 1]).astype(jnp.bfloat16)
        dims = (((1,), (1 if forward else 0,)), ((), ()))
        term = lax.dot_general(khatri, activity_ref[0, k], dims, preferred_element_type=jnp.float32)
        total = term if total is None else total + term
    width = outputs[0].shape[1]
    for q in range(count):
        sums_ref[q] = total[:, q * width : (q + 1) * width]
    for d, out in enumerate(outputs):
        out[...] = sums_ref[me ^ d]


def tile_sums(activity, pieces, time_factor, forward):
    count = len(pieces)
    rank = time_factor.shape[1]
    _, steps, rows, cols = activity.shape
    width = (rows if forward else cols) // count
    return kernel_call(
        functools.partial(tile_kernel, forward, count), [shape((rank, width))] * count,
        activity, time_factor, *pieces,
        scratch=[
            pltpu.VMEM((count, *pieces[0].shape), jnp.bfloat16),
            pltpu.VMEM((count, rank, width), jnp.float32),
        ],
        flops=2 * rank * steps * rows * cols,
    )


def place_kernel(count, table_ref, *refs):
    received, outputs = refs[:count], refs[count:]
    values = [x[...] for x in received]
    for r, out in enumerate(outputs):
        total = None
        for d, value in enumerate(values):
            here = jnp.broadcast_to(table_ref[d : d + 1, :1] == r, value.shape)
            term = jnp.where(here, value, 0.0)
            total = term if total is None else total + term
        out[...] = total


def owner_sums(partials, table):
    received = swaps(partials)
    size = lax.axis_size("wide")
    placed = kernel_call(
        functools.partial(place_kernel, len(received)), [shape(received[0].shape)] * size,
        table, *received,
    )
    order = list(reversed(range(1, size // 2)))
    arrived = {m: swap(placed[2 * m + 1], "wide", 1) for m in order}
    terms = [placed[0], swap(placed[1], "wide", 1)]
    for m in order:
        terms.append(swap(placed[2 * m] + arrived[m], "wide", 2 * m))
    return terms


def update_kernel(terms, count, *refs):
    sums = refs[0][...]
    for term in refs[1:terms]:
        sums = sums + term[...]
    shifted_ref, dual_ref, penalty_ref, inverse_ref = refs[terms : terms + 4]
    outputs = refs[terms + 4 :]
    value_ref = outputs[-1]
    penalty = penalty_ref[:1, :1]
    inverse = inverse_ref[...]
    shifted, dual = shifted_ref[...], dual_ref[...]
    for _ in range(PASSES):
        target = jnp.dot(
            inverse, sums + penalty * shifted, precision=HIGHEST, preferred_element_type=jnp.float32
        )
        value = target - dual
        dual = jnp.maximum(-value, 0.0)
        shifted = jnp.abs(value)
    value_ref[...] = value
    height = outputs[0].shape[0]
    for d in range(count):
        outputs[d][...] = value_ref[rows_of(d, height), :]
    if len(outputs) > count + 1:
        store_pair(jnp.maximum(value, 0.0), outputs[count])


def admm(terms, shifted, dual, penalty, inverse, more):
    count = lax.axis_size("narrow")
    rank, width = shifted.shape
    out = [shape((rank // count, width))] * count
    if more:
        out += [shape((2 * rank, width), jnp.bfloat16)]
    return kernel_call(
        functools.partial(update_kernel, len(terms), count), out,
        *terms, shifted, dual, penalty, inverse,
        scratch=[pltpu.VMEM((rank, width), jnp.float32)],
        flops=12 * rank * rank * width * PASSES,
    )


def final_kernel(count, *refs):
    pieces, (factor_ref, dual_ref) = refs[:count], refs[count:]
    width = pieces[0].shape[1]

    def body(v):
        for d, piece in enumerate(pieces):
            lanes = slice((v ^ d) * width, ((v ^ d) + 1) * width)
            value = piece[...]
            factor_ref[:, lanes] = jnp.maximum(value, 0.0)
            dual_ref[:, lanes] = jnp.maximum(-value, 0.0)

    for_each_position(body)


def to_columns(pieces):
    received = swaps(pieces)
    height, width = received[0].shape
    count = len(received)
    factor, dual = kernel_call(
        functools.partial(final_kernel, count), [shape((height, count * width))] * 2,
        *received,
    )
    return factor.T, dual.T


def local(
    activity,
    tile_coords,
    user_owner,
    item_owner,
    user_factor,
    item_factor,
    time_factor,
    user_dual,
    item_dual,
):
    return sweep(
        activity, tile_coords, user_owner, item_owner, user_factor.T, item_factor.T,
        time_factor, user_dual.T, item_dual.T,
    )


def sweep(
    activity, tile_coords, user_owner, item_owner, user_factor, item_factor, time_factor,
    user_dual, item_dual,
):
    rank = time_factor.shape[1]
    count = lax.axis_size("narrow")
    user_table, item_table = positions(tile_coords, user_owner, item_owner)

    pieces = swaps(split(item_factor))
    rows = shape((rank, pieces[0].shape[1]))
    pair = shape((2 * rank, rows.shape[1]), jnp.bfloat16)
    item_rows, pair = kernel_call(functools.partial(pair_kernel, count), [rows, pair], *pieces)
    stack = jnp.concatenate([user_factor, user_dual, item_dual])
    user_shifted, udual_rows, item_shifted, idual_rows = kernel_call(
        functools.partial(assemble_kernel, count), [rows] * 4,
        item_rows, *swaps(split(stack)),
    )

    pairs = all_pairs(pair)
    partials = tile_sums(activity, fetch_rows(pairs, item_table), time_factor, True)
    terms = owner_sums(partials, user_table)
    penalty, inverse = penalty_inverse(joint_gram(pairs), time_factor)
    *user_pieces, pair = admm(terms, user_shifted, udual_rows, penalty, inverse, True)

    pairs = all_pairs(pair)
    partials = tile_sums(activity, fetch_rows(pairs, user_table), time_factor, False)
    terms = owner_sums(partials, item_table)
    penalty, inverse = penalty_inverse(joint_gram(pairs), time_factor)
    new_users, new_user_dual = to_columns(user_pieces)
    item_pieces = admm(terms, item_shifted, idual_rows, penalty, inverse, False)
    new_items, new_item_dual = to_columns(item_pieces)
    return (new_users, new_items, new_user_dual, new_item_dual)


def solution(mesh):
    in_specs = (
        P(("wide", "narrow"), None, None, None),
        P(),
        P(),
        P(),
        P("wide", "narrow"),
        P("wide", "narrow"),
        P(),
        P("wide", "narrow"),
        P("wide", "narrow"),
    )
    out_specs = (P("wide", "narrow"), P("wide", "narrow"), P("wide", "narrow"), P("wide", "narrow"))
    return jax.shard_map(local, mesh=mesh, in_specs=in_specs, out_specs=out_specs, check_vma=False)
```
